512 devices in a mesh: heads: 8 (over z), seq: 64 (over x, y, core).
Axes of the slice: x: 4, y: 8, z: 8, core: 2. Of those that a mesh axis runs over, the one named last changes fastest.
Arguments:
- queries: bfloat16 [32768, 4096], P('seq', 'heads'), may hold values from -6 to 6
- key_vectors: bfloat16 [32768, 4096], P('seq', 'heads'), may hold values from -6 to 6
- values: bfloat16 [32768, 4096], P('seq', 'heads'), may hold values from -40 to 40
- level_weights: float32 [16, 32, 32768], P(None, 'heads', 'seq'), may hold values from 0.1 to 1
- gate_branch: bfloat16 [32768, 4096], P(('seq', 'heads')), may hold values from -6 to 6
- norm_gain: float32 [4096], replicated, may hold values from 0.5 to 1.5
Outputs:
- normed: bfloat16 [32768, 4096], P(('seq', 'heads'))
The draws below stay inside these ranges and needn't reach their ends.
All inputs are finite; a program needn't handle non-finite values.
Results may differ from the reference program's by a relative error of at most 0.008.
Values may be sent and summed in bfloat16 or wider, within the bound.
A program may use at most 64 MiB of HBM per device.

```python
import math
import jax
import jax.numpy as jnp
from jax import lax

HEADS = 32
HEAD_DIM = 128
WINDOW = 512
TOK_DEV = 512
MODEL = 4096
TOKENS = 32768
NEAR_LEVELS = 10
FAR_LEVELS = 6
LEVELS = 16


def draw_queries(key, part):
    noise_key = jax.random.fold_in(key, 1)
    field = jnp.clip(1.4 * jax.random.normal(noise_key, (TOKENS, MODEL), jnp.float32), -6.0, 6.0)
    return field.astype(jnp.bfloat16)


def draw_key_vectors(key, part):
    noise_key = jax.random.fold_in(key, 2)
    field = jnp.clip(1.4 * jax.random.normal(noise_key, (TOKENS, MODEL), jnp.float32), -6.0, 6.0)
    return field.astype(jnp.bfloat16)


def draw_values(key, part):
    noise_key = jax.random.fold_in(key, 3)
    field = jnp.clip(jax.random.normal(noise_key, (TOKENS, MODEL), jnp.float32), -6.0, 6.0)
    return field.astype(jnp.bfloat16)


def level_of(stream_key, dims, cuts, least, largest):
    def one(dim, blocks):
        steps = jax.random.uniform(jax.random.fold_in(jax.random.fold_in(stream_key, 6), dim), (blocks,), jnp.float32, least / len(cuts), largest / len(cuts))
        return jnp.repeat(jnp.exp(steps), dims[dim] // blocks).reshape((-1,) + (1,) * (len(dims) - dim - 1))

    factor_of = one(*cuts[0])
    for cut in cuts[1:]:
        factor_of = factor_of * one(*cut)
    return factor_of


def gaussian(stream_key, shape, spread, most, pieces=(), held_as=jnp.bfloat16):
    values = jax.random.normal(stream_key, shape, jnp.float32) * spread
    if len(pieces) > 0:
        values = level_of(stream_key, shape, pieces, -0.22, 0.18) * values
    return jnp.clip(values, min=-most, max=most).astype(held_as)


def setup_inputs(seed: int = 0) -> dict:
    splits = jax.random.split(jax.random.key(seed), 7)
    return {
        "queries": draw_queries(jax.random.fold_in(splits[6], 71), 0),
        "key_vectors": draw_key_vectors(jax.random.fold_in(splits[6], 71), 0),
        "values": draw_values(jax.random.fold_in(splits[6], 71), 0),
        "level_weights": jnp.clip(jnp.exp(math.log(1.0) - 2.3025851 * jax.random.uniform(splits[3], (LEVELS, HEADS, TOKENS), jnp.float32) ** level_of(splits[3], (LEVELS, HEADS, TOKENS), ((1, 8), (2, 64)), -0.2, 0.2)), 0.1, 1.0),
        "gate_branch": gaussian(splits[4], (TOKENS, MODEL), 1.0, 6.0, ((0, 512),)),
        "norm_gain": jnp.clip(1.0 + 0.1 * jax.random.normal(splits[5], (MODEL,), jnp.float32), 0.5, 1.5),
    }


EPSILON = 1e-06

def bit_count(numbers, width_bits):
    lengths = jnp.zeros(numbers.shape, jnp.int32)
    for shift_bit in range(width_bits):
        lengths = lengths + (numbers >> shift_bit > 0).astype(jnp.int32)
    return lengths

def level_scale(levels):
    return jnp.exp2(-0.5 * jnp.maximum(levels - 1, 0).astype(jnp.float32))

def reference(queries, key_vectors, values, level_weights, gate_branch, norm_gain):
    block_count = TOKENS // TOK_DEV
    score_scale = HEAD_DIM ** (-0.5)
    positions = jnp.arange(TOK_DEV, dtype=jnp.int32)
    level_table = bit_count(positions[:, None] ^ positions[None, :], NEAR_LEVELS)
    causal = positions[:, None] >= positions[None, :]
    near_scale = level_scale(jnp.arange(NEAR_LEVELS, dtype=jnp.int32))
    far_scale = level_scale(NEAR_LEVELS + jnp.arange(FAR_LEVELS, dtype=jnp.int32)) * score_scale
    block_ids = jnp.arange(block_count, dtype=jnp.int32)
    context_pos = jnp.arange(WINDOW + TOK_DEV, dtype=jnp.int32)

    def one_head(operands):
        query_head, key_head, value_head, weight_head = operands
        key_blocks = key_head.reshape(block_count, TOK_DEV, HEAD_DIM).astype(jnp.float32)
        value_blocks = value_head.reshape(block_count, TOK_DEV, HEAD_DIM).astype(jnp.float32)
        block_states = jnp.einsum('btd,bte->bde', key_blocks, value_blocks, precision=lax.Precision.HIGHEST).astype(jnp.bfloat16)
        state_float = lax.optimization_barrier(block_states).astype(jnp.float32)
        bucket_list = []
        for level_id in range(FAR_LEVELS):
            group_size = 2 ** level_id
            group_sums = state_float.reshape(block_count // group_size, group_size, HEAD_DIM, HEAD_DIM).sum(axis=1)
            sibling = jnp.maximum((block_ids >> level_id) - 1, 0)
            present = (block_ids >> level_id & 1).astype(jnp.float32)
            bucket_list.append(group_sums[sibling] * present[:, None, None])
        buckets = jnp.stack(bucket_list, axis=1).astype(jnp.bfloat16)
        padded_keys = jnp.concatenate([jnp.zeros((WINDOW, HEAD_DIM), jnp.bfloat16), key_head], axis=0)
        padded_values = jnp.concatenate([jnp.zeros((WINDOW, HEAD_DIM), jnp.bfloat16), value_head], axis=0)

        def one_block(block_id):
            first_token = block_id * TOK_DEV
            query_block = lax.dynamic_slice_in_dim(query_head, first_token, TOK_DEV, 0)
            context_keys = lax.dynamic_slice_in_dim(padded_keys, first_token, WINDOW + TOK_DEV, 0)
            context_values = lax.dynamic_slice_in_dim(padded_values, first_token, WINDOW + TOK_DEV, 0)
            block_weights = lax.dynamic_slice_in_dim(weight_head, first_token, TOK_DEV, 1)
            scores = jnp.dot(query_block, context_keys.T, preferred_element_type=jnp.float32) * score_scale
            key_pos = first_token - WINDOW + context_pos
            pos_gap = positions[:, None] + WINDOW - context_pos[None, :]
            in_window = (pos_gap >= 0) & (pos_gap < WINDOW) & (key_pos >= 0)[None, :]
            row_max = lax.optimization_barrier(jnp.max(jnp.where(in_window, scores, -jnp.inf), axis=1, keepdims=True))
            exp_scores = jnp.where(in_window, jnp.exp(scores - row_max), 0.0)
            weights = (exp_scores / lax.optimization_barrier(jnp.sum(exp_scores, axis=1, keepdims=True))).astype(jnp.bfloat16)
            windowed = jnp.dot(weights, context_values, preferred_element_type=jnp.float32)
            level_mix = jnp.zeros((TOK_DEV, TOK_DEV), jnp.float32)
            for level_id in range(NEAR_LEVELS):
                level_mix = level_mix + jnp.where(level_table == level_id, (block_weights[level_id] * near_scale[level_id])[:, None], 0.0)
            level_mix = jnp.where(causal, level_mix, 0.0)
            near_weights = (scores[:, WINDOW:] * level_mix).astype(jnp.bfloat16)
            near_out = jnp.dot(near_weights, context_values[WINDOW:], preferred_element_type=jnp.float32)
            block_buckets = buckets[block_id]
            far_proj = jnp.einsum('td,jde->jte', query_block.astype(jnp.float32), block_buckets.astype(jnp.float32), precision=lax.Precision.HIGHEST)
            far_coef = block_weights[NEAR_LEVELS:] * far_scale[:, None]
            far_out = lax.optimization_barrier(jnp.sum(far_coef[:, :, None] * far_proj, axis=0))
            return windowed + near_out + far_out
        return lax.map(one_block, block_ids).reshape(TOKENS, HEAD_DIM)
    query_heads = queries.reshape(TOKENS, HEADS, HEAD_DIM).transpose(1, 0, 2)
    key_heads = key_vectors.reshape(TOKENS, HEADS, HEAD_DIM).transpose(1, 0, 2)
    value_heads = values.reshape(TOKENS, HEADS, HEAD_DIM).transpose(1, 0, 2)
    head_outputs = lax.map(one_head, (query_heads, key_heads, value_heads, level_weights.transpose(1, 0, 2)))
    mixed = head_outputs.transpose(1, 0, 2).reshape(TOKENS, MODEL).astype(jnp.bfloat16)
    gated = mixed.astype(jnp.float32) * jax.nn.silu(gate_branch.astype(jnp.float32))
    mean_square = lax.optimization_barrier(jnp.mean(gated * gated, axis=1, keepdims=True))
    return (norm_gain * gated * lax.rsqrt(mean_square + EPSILON)).astype(jnp.bfloat16)
```

```python
import functools
import math

import jax
import jax.numpy as jnp
from jax import lax
from jax.experimental import pallas as pl
from jax.experimental.pallas import tpu as pltpu
from jax.sharding import PartitionSpec as P

HEAD_DIM = 128
EPSILON = 1e-06
NEAR_LEVELS = 10
FAR_LEVELS = 6
TILE = 128
MESH = pl.DeviceIdType.MESH
F32 = jnp.float32
BF16 = jnp.bfloat16
SCALE = HEAD_DIM**-0.5
NEG = -1e30


def level_scale(level):
    return 2.0 ** (-0.5 * max(level - 1, 0))


def dot_nt(a, b):
    return lax.dot_general(a, b, (((1,), (1,)), ((), ())), preferred_element_type=F32)


def dot_nn(a, b):
    return jnp.dot(a, b, preferred_element_type=F32)


def kernel(
    rows_x,
    rows_y,
    groups,
    q_hbm,
    k_hbm,
    v_hbm,
    lw_hbm,
    gate_hbm,
    gain_ref,
    out_ref,
    q,
    k,
    v,
    vt,
    kp,
    vpt,
    lw,
    gate,
    silu,
    acc,
    mix,
    tok,
    st,
    gat,
    bsrc,
    tsrc,
    tbuf,
    xsrc,
    bk,
    q_sem,
    k_sem,
    v_sem,
    lw_sem,
    gate_sem,
    a_send,
    a_recv,
    z_send,
    z_recv,
    ks_send,
    ks_recv,
    vs_send,
    vs_recv,
    t_send,
    t_recv,
    c_send,
    c_recv,
    h_send,
    h_recv,
    o_send,
    o_recv,
):
    heads = k.shape[0]
    toks = k.shape[1]
    tiles = toks // TILE
    row_n = rows_y * 2
    seq_n = rows_x * row_n
    half = heads * HEAD_DIM // 2
    part = half // rows_y
    out_rows = toks // groups
    me = lax.axis_index("seq")
    zed = lax.axis_index("heads")
    x = me // row_n
    r = lax.rem(me, row_n)
    y = r // 2
    c = lax.rem(r, 2)

    def head_at(core, step):
        return lax.rem(core * (heads // 2) + step, heads)

    def row_id(place):
        return x * row_n + place

    loads = []
    for h in range(heads):
        cols = pl.ds(h * HEAD_DIM, HEAD_DIM)
        for src, dst, sem in ((k_hbm, k, k_sem), (v_hbm, v, v_sem), (q_hbm, q, q_sem)):
            copy = pltpu.make_async_copy(src.at[:, cols], dst.at[h], sem.at[h])
            copy.start()
            loads.append(copy)
    lw_copies = [
        pltpu.make_async_copy(lw_hbm.at[:, pl.ds(h, 1), :], lw.at[h], lw_sem.at[h])
        for h in range(heads)
    ]
    for copy in lw_copies:
        copy.start()
    gate_copy = pltpu.make_async_copy(gate_hbm, gate, gate_sem)
    gate_copy.start()

    barrier = pltpu.get_barrier_semaphore()
    after = lax.rem(me + 1, seq_n)
    before = lax.rem(me + seq_n - 1, seq_n)
    greeted = 0
    for place in (after, before):
        pl.semaphore_signal(barrier, inc=1, device_id={"seq": place}, device_id_type=MESH)
        greeted += 1
    for step in range(1, row_n):
        pl.semaphore_signal(
            barrier,
            inc=1,
            device_id={"seq": row_id(lax.rem(r + step, row_n))},
            device_id_type=MESH,
        )
        greeted += 1
    for step in range(1, rows_x):
        pl.semaphore_signal(
            barrier,
            inc=1,
            device_id={"seq": lax.rem(x + step, rows_x) * row_n + r},
            device_id_type=MESH,
        )
        greeted += 1
    for step in range(1, groups):
        pl.semaphore_signal(
            barrier,
            inc=1,
            device_id={"heads": lax.rem(zed + step, groups)},
            device_id_type=MESH,
        )
        greeted += 1

    for h in range(heads):
        pltpu.make_async_copy(k_hbm.at[:, pl.ds(0, HEAD_DIM)], k.at[h], k_sem.at[h]).wait()
        pltpu.make_async_copy(v_hbm.at[:, pl.ds(0, HEAD_DIM)], v.at[h], v_sem.at[h]).wait()
        turned = v[h].T
        vt[h] = turned
        st[pl.ds(h * HEAD_DIM, HEAD_DIM), :] = dot_nn(turned, k[h]).astype(BF16)

    pl.semaphore_wait(barrier, greeted)

    for step in range(1, row_n):
        place = lax.rem(r + step, row_n)
        rows = pl.multiple_of(lax.rem(place, 2) * half + (place // 2) * part, part)
        pltpu.make_async_remote_copy(
            st.at[pl.ds(rows, part), :],
            gat.at[r],
            a_send,
            a_recv,
            device_id={"seq": row_id(place)},
            device_id_type=MESH,
        ).start()
    mine = pl.multiple_of(c * half + y * part, part)
    gat[r] = st[pl.ds(mine, part), :]

    sibling = me + 1 - 2 * c

    @pl.when(c == 0)
    def _():
        pltpu.make_async_remote_copy(
            st, bk.at[0], z_send, z_recv, device_id={"seq": sibling}, device_id_type=MESH
        ).start()

    def send_window(step, carry):
        h = head_at(1 - c, step)
        pltpu.make_async_remote_copy(
            k.at[h],
            kp.at[h],
            ks_send.at[step],
            ks_recv.at[step],
            device_id={"seq": after},
            device_id_type=MESH,
        ).start()
        pltpu.make_async_remote_copy(
            vt.at[h],
            vpt.at[h],
            vs_send.at[step],
            vs_recv.at[step],
            device_id={"seq": after},
            device_id_type=MESH,
        ).start()
        return carry

    lax.fori_loop(0, heads, send_window, 0)

    @pl.when(c == 0)
    def _():
        bk[0] = jnp.zeros(bk.shape[1:], BF16)

    def bit_of(level):
        return lax.rem(me // (1 << level), 2)

    for level in range(1, FAR_LEVELS):

        @pl.when(bit_of(level) == 0)
        def _():
            bk[level] = jnp.zeros(bk.shape[1:], BF16)

    gate_copy.wait()
    wide = gate[...].astype(F32)
    silu[...] = wide * jax.nn.sigmoid(wide)

    pltpu.make_async_copy(
        gat.at[pl.ds(0, row_n - 1)], gat.at[pl.ds(0, row_n - 1)], a_recv
    ).wait()
    sums = [gat[i].astype(F32) for i in range(row_n)]
    level_sums = []
    while len(sums) > 1:
        sums = [sums[2 * i] + sums[2 * i + 1] for i in range(len(sums) // 2)]
        level_sums.append(sums)
    low_levels = len(level_sums) - 1
    firsts = []
    count = 0
    for level_list in level_sums[:-1]:
        firsts.append(count)
        for i in range(0, len(level_list), 2):
            bsrc[count] = level_list[i].astype(BF16)
            count += 1
    total = level_sums[-1][0]
    tsrc[...] = total
    tbuf[x] = total
    for step in range(1, rows_x):
        pltpu.make_async_remote_copy(
            tsrc,
            tbuf.at[x],
            t_send,
            t_recv,
            device_id={"seq": lax.rem(x + step, rows_x) * row_n + r},
            device_id_type=MESH,
        ).start()
    for level in range(low_levels, 0, -1):
        for step in (4, 3, 5, 2, 6, 1, 7, 0):
            place = lax.rem(y + step, rows_y)
            src = bsrc.at[firsts[level - 1] + place // (1 << level)]
            dst = bk.at[level, pl.ds(mine, part), :]

            @pl.when(lax.rem(place // (1 << (level - 1)), 2) == 1)
            def _():
                if step == 0:
                    pltpu.make_async_copy(src, dst, c_recv.at[level]).start()
                else:
                    pltpu.make_async_remote_copy(
                        src,
                        dst,
                        c_send.at[level],
                        c_recv.at[level],
                        device_id={"seq": row_id(place * 2 + c)},
                        device_id_type=MESH,
                    ).start()

    for h in range(heads):
        pltpu.make_async_copy(q_hbm.at[:, pl.ds(0, HEAD_DIM)], q.at[h], q_sem.at[h]).wait()
    for copy in lw_copies:
        copy.wait()
    key_at = lax.broadcasted_iota(jnp.int32, (TILE, TILE), 0)
    query_at = lax.broadcasted_iota(jnp.int32, (TILE, TILE), 1)
    gain_exp = SCALE * math.log2(math.e)

    def window(step, carry):
        h = head_at(c, step)
        pltpu.make_async_copy(k.at[h], kp.at[h], ks_recv.at[step]).wait()
        pltpu.make_async_copy(vt.at[h], vpt.at[h], vs_recv.at[step]).wait()
        causal = key_at <= query_at
        apart = key_at ^ query_at
        for i in range(tiles):
            cols = pl.ds(i * TILE, TILE)
            query = q[h, cols, :]
            own = dot_nt(k[h, pl.ds(0, (i + 1) * TILE), :], query)
            past = dot_nt(kp[h, pl.ds(i * TILE, toks - i * TILE), :], query)
            past = jnp.where(me == 0, NEG, past)
            own_tiles = [own[j * TILE : (j + 1) * TILE] for j in range(i + 1)]
            past_tiles = [past[j * TILE : (j + 1) * TILE] for j in range(tiles - i)]
            both = own_tiles[:-1] + [jnp.where(causal, own_tiles[-1], past_tiles[0])] + past_tiles[1:]
            top = functools.reduce(jnp.maximum, both)
            top = jnp.max(top, axis=0, keepdims=True) * gain_exp
            powers = [jnp.exp2(tile * gain_exp - top) for tile in both]
            mass = jnp.sum(functools.reduce(jnp.add, powers), axis=0, keepdims=True)
            share = 1.0 / mass
            weights = [power * share for power in powers]
            rows = [
                lw[h, level, :, cols] * (level_scale(level) * SCALE)
                for level in range(NEAR_LEVELS)
            ]
            own_weights = []
            for j in range(i):
                level = TILE.bit_length() - 1 + (i ^ j).bit_length()
                own_weights.append((weights[j] + own_tiles[j] * rows[level]).astype(BF16))
            mixed = jnp.broadcast_to(rows[0], (TILE, TILE))
            for level in range(1, TILE.bit_length()):
                mixed = jnp.where(apart >= 1 << (level - 1), rows[level], mixed)
            own_weights.append(
                jnp.where(causal, weights[i] + own_tiles[i] * mixed, 0.0).astype(BF16)
            )
            past_weights = [jnp.where(causal, 0.0, weights[i]).astype(BF16)]
            past_weights += [weight.astype(BF16) for weight in weights[i + 1 :]]
            found = dot_nn(vt[h, :, pl.ds(0, (i + 1) * TILE)], jnp.concatenate(own_weights, axis=0))
            found += dot_nn(
                vpt[h, :, pl.ds(i * TILE, toks - i * TILE)], jnp.concatenate(past_weights, axis=0)
            )
            acc[h, :, cols] = found
        return carry

    window(0, 0)

    pltpu.make_async_copy(
        tbuf.at[pl.ds(0, rows_x - 1)], tbuf.at[pl.ds(0, rows_x - 1)], t_recv
    ).wait()
    xsrc[0] = tbuf[lax.max(x - 1, 0)].astype(BF16)
    xsrc[1] = (tbuf[0] + tbuf[1]).astype(BF16)
    for up in range(FAR_LEVELS - 1 - low_levels):
        level = low_levels + 1 + up

        @pl.when(bit_of(level) == 1)
        def _():
            for step in (4, 3, 5, 2, 6, 1, 7, 0):
                place = lax.rem(y + step, rows_y)
                src = xsrc.at[up]
                dst = bk.at[level, pl.ds(mine, part), :]
                if step == 0:
                    pltpu.make_async_copy(src, dst, c_recv.at[level]).start()
                else:
                    pltpu.make_async_remote_copy(
                        src,
                        dst,
                        c_send.at[level],
                        c_recv.at[level],
                        device_id={"seq": row_id(place * 2 + c)},
                        device_id_type=MESH,
                    ).start()

    lax.fori_loop(1, heads, window, 0)

    my_half = pl.ds(pl.multiple_of(c * half, half), half)
    other_half = pl.ds(pl.multiple_of((1 - c) * half, half), half)
    for level in range(1, FAR_LEVELS):

        @pl.when(bit_of(level) == 1)
        def _():
            piece = bk.at[level, my_half, :]
            pltpu.make_async_copy(piece, piece, c_recv.at[level]).wait()
            pltpu.make_async_remote_copy(
                piece,
                piece,
                h_send.at[level],
                h_recv.at[level],
                device_id={"seq": sibling},
                device_id_type=MESH,
            ).start()

    @pl.when(c == 1)
    def _():
        pltpu.make_async_copy(st, bk.at[0], z_recv).wait()

    wide_cols = min(2 * TILE, toks)

    def far(step, carry):
        h = head_at(c, step)

        @pl.when(step == heads // 2)
        def _():
            for level in range(1, FAR_LEVELS):

                @pl.when(bit_of(level) == 1)
                def _():
                    piece = bk.at[level, other_half, :]
                    pltpu.make_async_copy(piece, piece, h_recv.at[level]).wait()

        rows = pl.ds(pl.multiple_of(h * HEAD_DIM, HEAD_DIM), HEAD_DIM)
        for start in range(0, toks, wide_cols):
            cols = pl.ds(start, wide_cols)
            query = q[h, cols, :]
            found = acc[h, :, cols]
            for level in range(FAR_LEVELS):
                weight = lw[h, NEAR_LEVELS + level, :, cols]
                weight = weight * (level_scale(NEAR_LEVELS + level) * SCALE)
                found += dot_nt(bk[level, rows, :], query) * weight
            mix[h, cols, :] = found.T.astype(BF16)
        for hop in (4, 3, 5, 2, 6, 1, 7):
            there = lax.rem(zed + hop, groups)
            pltpu.make_async_remote_copy(
                mix.at[h, pl.ds(pl.multiple_of(there * out_rows, out_rows), out_rows), :],
                tok.at[zed * heads + h],
                o_send.at[step],
                o_recv.at[step],
                device_id={"heads": there},
                device_id_type=MESH,
            ).start()
        tok[zed * heads + h] = mix[h, pl.ds(pl.multiple_of(zed * out_rows, out_rows), out_rows), :]
        return carry

    lax.fori_loop(0, heads, far, 0)

    lanes = jnp.zeros((out_rows, HEAD_DIM), F32)
    for step in range(heads):
        piece = tok.at[pl.ds(0, groups - 1)]
        pltpu.make_async_copy(piece, piece, o_recv.at[step]).wait()
        h = head_at(c, step)
        for group in range(groups):
            index = group * heads + h
            cols = pl.ds(pl.multiple_of(index * HEAD_DIM, HEAD_DIM), HEAD_DIM)
            gated = tok[index].astype(F32) * silu[:, cols]
            silu[:, cols] = gated
            lanes += gated * gated
    square = jnp.sum(lanes, axis=1, keepdims=True) * (1.0 / (groups * heads * HEAD_DIM))
    inverse = lax.rsqrt(square + EPSILON)
    for index in range(groups * heads):
        cols = pl.ds(index * HEAD_DIM, HEAD_DIM)
        out_ref[:, cols] = (gain_ref[:, cols] * silu[:, cols] * inverse).astype(BF16)

    piece = gat.at[pl.ds(0, row_n - 1)]
    pltpu.make_async_copy(piece, piece, a_send).wait()

    @pl.when(c == 0)
    def _():
        pltpu.make_async_copy(st, st, z_send).wait()

    for step in range(heads):
        pltpu.make_async_copy(k.at[0], k.at[0], ks_send.at[step]).wait()
        pltpu.make_async_copy(vt.at[0], vt.at[0], vs_send.at[step]).wait()
        piece = tok.at[pl.ds(0, groups - 1)]
        pltpu.make_async_copy(piece, piece, o_send.at[step]).wait()
    piece = tbuf.at[pl.ds(0, rows_x - 1)]
    pltpu.make_async_copy(piece, piece, t_send).wait()
    for level in range(1, FAR_LEVELS):
        if level <= low_levels:
            for own_bit in range(2):

                @pl.when(bit_of(level) == own_bit)
                def _():
                    piece = gat.at[pl.ds(0, rows_y // 2 - own_bit)]
                    pltpu.make_async_copy(piece, piece, c_send.at[level]).wait()

        else:

            @pl.when(bit_of(level) == 1)
            def _():
                piece = gat.at[pl.ds(0, rows_y - 1)]
                pltpu.make_async_copy(piece, piece, c_send.at[level]).wait()

        @pl.when(bit_of(level) == 1)
        def _():
            piece = bk.at[level, my_half, :]
            pltpu.make_async_copy(piece, piece, h_send.at[level]).wait()


def local(rows_x, rows_y, queries, key_vectors, values, level_weights, gate_branch, norm_gain):
    toks, width = queries.shape
    heads = width // HEAD_DIM
    groups = lax.axis_size("heads")
    out_rows, model = gate_branch.shape
    row_n = rows_y * 2
    part = heads * HEAD_DIM // row_n
    dma = pltpu.SemaphoreType.DMA
    hbm = pl.BlockSpec(memory_space=pl.ANY)
    vmem = pl.BlockSpec(memory_space=pltpu.VMEM)
    head_shape = (heads, toks, HEAD_DIM)
    turned_shape = (heads, HEAD_DIM, toks)
    return pl.pallas_call(
        functools.partial(kernel, rows_x, rows_y, groups),
        out_shape=jax.ShapeDtypeStruct((out_rows, model), BF16),
        in_specs=[hbm] * 5 + [vmem],
        out_specs=vmem,
        scratch_shapes=[
            pltpu.VMEM(head_shape, BF16),
            pltpu.VMEM(head_shape, BF16),
            pltpu.VMEM(head_shape, BF16),
            pltpu.VMEM(turned_shape, BF16),
            pltpu.VMEM(head_shape, BF16),
            pltpu.VMEM(turned_shape, BF16),
            pltpu.VMEM((heads, level_weights.shape[0], 1, toks), F32),
            pltpu.VMEM(gate_branch.shape, BF16),
            pltpu.VMEM(gate_branch.shape, F32),
            pltpu.VMEM(turned_shape, F32),
            pltpu.VMEM(head_shape, BF16),
            pltpu.VMEM((groups * heads, out_rows, HEAD_DIM), BF16),
            pltpu.VMEM((heads * HEAD_DIM, HEAD_DIM), BF16),
            pltpu.VMEM((row_n, part, HEAD_DIM), BF16),
            pltpu.VMEM((row_n // 2 - 1, part, HEAD_DIM), BF16),
            pltpu.VMEM((part, HEAD_DIM), F32),
            pltpu.VMEM((rows_x, part, HEAD_DIM), F32),
            pltpu.VMEM((2, part, HEAD_DIM), BF16),
            pltpu.VMEM((FAR_LEVELS, heads * HEAD_DIM, HEAD_DIM), BF16),
            dma((heads,)),
            dma((heads,)),
            dma((heads,)),
            dma((heads,)),
            dma,
            dma,
            dma,
            dma,
            dma,
            dma((heads,)),
            dma((heads,)),
            dma((heads,)),
            dma((heads,)),
            dma,
            dma,
            dma((FAR_LEVELS,)),
            dma((FAR_LEVELS,)),
            dma((FAR_LEVELS,)),
            dma((FAR_LEVELS,)),
            dma((heads,)),
            dma((heads,)),
        ],
        compiler_params=pltpu.CompilerParams(
            collective_id=0, has_side_effects=True, vmem_limit_bytes=40 << 20
        ),
        name="layer",
    )(queries, key_vectors, values, level_weights, gate_branch, norm_gain.reshape(1, -1))


def solution(mesh):
    rows_x, rows_y = 4, 8
    return jax.shard_map(
        functools.partial(local, rows_x, rows_y),
        mesh=mesh,
        in_specs=(
            P("seq", "heads"),
            P("seq", "heads"),
            P("seq", "heads"),
            P(None, "heads", "seq"),
            P(("seq", "heads"), None),
            P(),
        ),
        out_specs=P(("seq", "heads"), None),
        check_vma=False,
    )
```

```python
import functools
import math

import jax
import jax.numpy as jnp
from jax import lax
from jax.experimental import pallas as pl
from jax.experimental.pallas import tpu as pltpu
from jax.sharding import PartitionSpec as P

HEAD_DIM = 128
EPSILON = 1e-06
NEAR_LEVELS = 10
FAR_LEVELS = 6
TILE = 128
MESH = pl.DeviceIdType.MESH
F32 = jnp.float32
BF16 = jnp.bfloat16
SCALE = HEAD_DIM**-0.5
NEG = -1e30


def level_scale(level):
    return 2.0 ** (-0.5 * max(level - 1, 0))


def dot_nt(a, b):
    return lax.dot_general(a, b, (((1,), (1,)), ((), ())), preferred_element_type=F32)


def dot_nn(a, b):
    return jnp.dot(a, b, preferred_element_type=F32)


def kernel(
    rows_x,
    rows_y,
    groups,
    q_hbm,
    k_hbm,
    v_hbm,
    lw_hbm,
    gate_hbm,
    gain_hbm,
    out_ref,
    q,
    k,
    v,
    vt,
    kp,
    vpt,
    lw,
    gate,
    silu,
    acc,
    mix,
    tok,
    st,
    gat,
    bsrc,
    tsrc,
    tbuf,
    xsrc,
    bk,
    gain_ref,
    q_sem,
    k_sem,
    v_sem,
    lw_sem,
    gate_sem,
    gain_sem,
    a_send,
    a_recv,
    z_send,
    z_recv,
    ks_send,
    ks_recv,
    vs_send,
    vs_recv,
    t_send,
    t_recv,
    c_send,
    c_recv,
    h_send,
    h_recv,
    o_send,
    o_recv,
    here_sem,
):
    heads = k.shape[0]
    toks = k.shape[1]
    tiles = toks // TILE
    row_n = rows_y * 2
    seq_n = rows_x * row_n
    half = heads * HEAD_DIM // 2
    part = half // rows_y
    out_rows = toks // groups
    me = lax.axis_index("seq")
    zed = lax.axis_index("heads")
    x = me // row_n
    r = lax.rem(me, row_n)
    y = r // 2
    c = lax.rem(r, 2)

    def head_at(core, step):
        return lax.rem(core * (heads // 2) + step, heads)

    def row_id(place):
        return x * row_n + place

    barrier = pltpu.get_barrier_semaphore()
    after = lax.rem(me + 1, seq_n)
    before = lax.rem(me + seq_n - 1, seq_n)
    greeted = 0
    for place in (after, before):
        pl.semaphore_signal(barrier, inc=1, device_id={"seq": place}, device_id_type=MESH)
        greeted += 1
    for step in range(1, row_n):
        pl.semaphore_signal(
            barrier,
            inc=1,
            device_id={"seq": row_id(lax.rem(r + step, row_n))},
            device_id_type=MESH,
        )
        greeted += 1
    for step in range(1, rows_x):
        pl.semaphore_signal(
            barrier,
            inc=1,
            device_id={"seq": lax.rem(x + step, rows_x) * row_n + r},
            device_id_type=MESH,
        )
        greeted += 1
    for step in range(1, groups):

        @pl.when(zed + step < groups)
        def _():
            pl.semaphore_signal(
                barrier, inc=1, device_id={"heads": zed + step}, device_id_type=MESH
            )


    loads = []
    for h in range(heads):
        cols = pl.ds(h * HEAD_DIM, HEAD_DIM)
        for src, dst, sem in ((k_hbm, k, k_sem), (v_hbm, v, v_sem), (q_hbm, q, q_sem)):
            copy = pltpu.make_async_copy(src.at[:, cols], dst.at[h], sem.at[h])
            copy.start()
            loads.append(copy)
    lw_copies = [
        pltpu.make_async_copy(lw_hbm.at[:, pl.ds(h, 1), :], lw.at[h], lw_sem.at[h])
        for h in range(heads)
    ]
    for copy in lw_copies:
        copy.start()
    gate_copy = pltpu.make_async_copy(gate_hbm, gate, gate_sem)
    gate_copy.start()
    gain_copy = pltpu.make_async_copy(gain_hbm, gain_ref, gain_sem)
    gain_copy.start()

    for h in range(heads):
        pltpu.make_async_copy(k_hbm.at[:, pl.ds(0, HEAD_DIM)], k.at[h], k_sem.at[h]).wait()
        pltpu.make_async_copy(v_hbm.at[:, pl.ds(0, HEAD_DIM)], v.at[h], v_sem.at[h]).wait()
        turned = v[h].T
        vt[h] = turned
        st[pl.ds(h * HEAD_DIM, HEAD_DIM), :] = dot_nn(turned, k[h]).astype(BF16)

    pl.semaphore_wait(barrier, greeted + zed)
    for step in range(1, groups):

        @pl.when(zed >= step)
        def _():
            pl.semaphore_signal(
                here_sem, inc=1, device_id={"heads": zed - step}, device_id_type=MESH
            )


    for step in range(1, row_n):
        place = lax.rem(r + step, row_n)
        rows = pl.multiple_of(lax.rem(place, 2) * half + (place // 2) * part, part)
        pltpu.make_async_remote_copy(
            st.at[pl.ds(rows, part), :],
            gat.at[r],
            a_send,
            a_recv,
            device_id={"seq": row_id(place)},
            device_id_type=MESH,
        ).start()
    mine = pl.multiple_of(c * half + y * part, part)
    gat[r] = st[pl.ds(mine, part), :]

    sibling = me + 1 - 2 * c

    @pl.when(c == 0)
    def _():
        pltpu.make_async_remote_copy(
            st, bk.at[0], z_send, z_recv, device_id={"seq": sibling}, device_id_type=MESH
        ).start()

    def send_window(step):
        h = head_at(1 - c, step)
        pltpu.make_async_remote_copy(
            k.at[h],
            kp.at[h],
            ks_send.at[step],
            ks_recv.at[step],
            device_id={"seq": after},
            device_id_type=MESH,
        ).start()
        pltpu.make_async_remote_copy(
            vt.at[h],
            vpt.at[h],
            vs_send.at[step],
            vs_recv.at[step],
            device_id={"seq": after},
            device_id_type=MESH,
        ).start()

    send_window(0)

    @pl.when(c == 0)
    def _():
        bk[0] = jnp.zeros(bk.shape[1:], BF16)

    def bit_of(level):
        return lax.rem(me // (1 << level), 2)

    for level in range(1, FAR_LEVELS):

        @pl.when(bit_of(level) == 0)
        def _():
            bk[level] = jnp.zeros(bk.shape[1:], BF16)

    gate_copy.wait()
    gain_copy.wait()
    wide = gate[...].astype(F32)
    silu[...] = wide * jax.nn.sigmoid(wide)

    pltpu.make_async_copy(
        gat.at[pl.ds(0, row_n - 1)], gat.at[pl.ds(0, row_n - 1)], a_recv
    ).wait()
    sums = [gat[i].astype(F32) for i in range(row_n)]
    level_sums = []
    while len(sums) > 1:
        sums = [sums[2 * i] + sums[2 * i + 1] for i in range(len(sums) // 2)]
        level_sums.append(sums)
    low_levels = len(level_sums) - 1
    firsts = []
    count = 0
    for level_list in level_sums[:-1]:
        firsts.append(count)
        for i in range(0, len(level_list), 2):
            bsrc[count] = level_list[i].astype(BF16)
            count += 1
    total = level_sums[-1][0]
    tsrc[...] = total
    tbuf[x] = total
    for step in range(1, rows_x):
        pltpu.make_async_remote_copy(
            tsrc,
            tbuf.at[x],
            t_send,
            t_recv,
            device_id={"seq": lax.rem(x + step, rows_x) * row_n + r},
            device_id_type=MESH,
        ).start()
    for level in range(low_levels, 0, -1):
        for step in (4, 3, 5, 2, 6, 1, 7, 0):
            place = lax.rem(y + step, rows_y)
            src = bsrc.at[firsts[level - 1] + place // (1 << level)]
            dst = bk.at[level, pl.ds(mine, part), :]

            @pl.when(lax.rem(place // (1 << (level - 1)), 2) == 1)
            def _():
                if step == 0:
                    pltpu.make_async_copy(src, dst, c_recv.at[level]).start()
                else:
                    pltpu.make_async_remote_copy(
                        src,
                        dst,
                        c_send.at[level],
                        c_recv.at[level],
                        device_id={"seq": row_id(place * 2 + c)},
                        device_id_type=MESH,
                    ).start()

    send_window(1)

    for h in range(heads):
        pltpu.make_async_copy(q_hbm.at[:, pl.ds(0, HEAD_DIM)], q.at[h], q_sem.at[h]).wait()
    for copy in lw_copies:
        copy.wait()
    key_at = lax.broadcasted_iota(jnp.int32, (TILE, TILE), 0)
    query_at = lax.broadcasted_iota(jnp.int32, (TILE, TILE), 1)
    gain_exp = SCALE * math.log2(math.e)

    def window(step):
        h = head_at(c, step)
        pltpu.make_async_copy(k.at[h], kp.at[h], ks_recv.at[step]).wait()
        pltpu.make_async_copy(vt.at[h], vpt.at[h], vs_recv.at[step]).wait()
        causal = key_at <= query_at
        apart = key_at ^ query_at
        for i in range(tiles):
            cols = pl.ds(i * TILE, TILE)
            query = q[h, cols, :]
            own = dot_nt(k[h, pl.ds(0, (i + 1) * TILE), :], query)
            past = dot_nt(kp[h, pl.ds(i * TILE, toks - i * TILE), :], query)
            past = jnp.where(me == 0, NEG, past)
            own_tiles = [own[j * TILE : (j + 1) * TILE] for j in range(i + 1)]
            past_tiles = [past[j * TILE : (j + 1) * TILE] for j in range(tiles - i)]
            both = own_tiles[:-1] + [jnp.where(causal, own_tiles[-1], past_tiles[0])] + past_tiles[1:]
            top = functools.reduce(jnp.maximum, both)
            top = jnp.max(top, axis=0, keepdims=True) * gain_exp
            powers = [jnp.exp2(tile * gain_exp - top) for tile in both]
            mass = jnp.sum(functools.reduce(jnp.add, powers), axis=0, keepdims=True)
            share = 1.0 / mass
            weights = [power * share for power in powers]
            rows = [
                lw[h, level, :, cols] * (level_scale(level) * SCALE)
                for level in range(NEAR_LEVELS)
            ]
            own_weights = []
            for j in range(i):
                level = TILE.bit_length() - 1 + (i ^ j).bit_length()
                own_weights.append((weights[j] + own_tiles[j] * rows[level]).astype(BF16))
            mixed = jnp.broadcast_to(rows[0], (TILE, TILE))
            for level in range(1, TILE.bit_length()):
                mixed = jnp.where(apart >= 1 << (level - 1), rows[level], mixed)
            own_weights.append(
                jnp.where(causal, weights[i] + own_tiles[i] * mixed, 0.0).astype(BF16)
            )
            past_weights = [jnp.where(causal, 0.0, weights[i]).astype(BF16)]
            past_weights += [weight.astype(BF16) for weight in weights[i + 1 :]]
            found = dot_nn(vt[h, :, pl.ds(0, (i + 1) * TILE)], jnp.concatenate(own_weights, axis=0))
            found += dot_nn(
                vpt[h, :, pl.ds(i * TILE, toks - i * TILE)], jnp.concatenate(past_weights, axis=0)
            )
            acc[h, :, cols] = found

    window(0)

    pltpu.make_async_copy(
        tbuf.at[pl.ds(0, rows_x - 1)], tbuf.at[pl.ds(0, rows_x - 1)], t_recv
    ).wait()
    xsrc[0] = tbuf[lax.max(x - 1, 0)].astype(BF16)
    xsrc[1] = (tbuf[0] + tbuf[1]).astype(BF16)
    for up in range(FAR_LEVELS - 1 - low_levels):
        level = low_levels + 1 + up

        @pl.when(bit_of(level) == 1)
        def _():
            for step in (4, 3, 5, 2, 6, 1, 7, 0):
                place = lax.rem(y + step, rows_y)
                src = xsrc.at[up]
                dst = bk.at[level, pl.ds(mine, part), :]
                if step == 0:
                    pltpu.make_async_copy(src, dst, c_recv.at[level]).start()
                else:
                    pltpu.make_async_remote_copy(
                        src,
                        dst,
                        c_send.at[level],
                        c_recv.at[level],
                        device_id={"seq": row_id(place * 2 + c)},
                        device_id_type=MESH,
                    ).start()

    for step in range(2, heads):
        send_window(step)
    window(1)

    my_half = pl.ds(pl.multiple_of(c * half, half), half)
    other_half = pl.ds(pl.multiple_of((1 - c) * half, half), half)
    for level in range(1, FAR_LEVELS):

        @pl.when(bit_of(level) == 1)
        def _():
            piece = bk.at[level, my_half, :]
            pltpu.make_async_copy(piece, piece, c_recv.at[level]).wait()
            pltpu.make_async_remote_copy(
                piece,
                piece,
                h_send.at[level],
                h_recv.at[level],
                device_id={"seq": sibling},
                device_id_type=MESH,
            ).start()

    @pl.when(c == 1)
    def _():
        pltpu.make_async_copy(st, bk.at[0], z_recv).wait()

    wide_cols = min(2 * TILE, toks)

    def far(step):
        h = head_at(c, step)

        rows = pl.ds(pl.multiple_of(h * HEAD_DIM, HEAD_DIM), HEAD_DIM)
        for start in range(0, toks, wide_cols):
            cols = pl.ds(start, wide_cols)
            query = q[h, cols, :]
            found = acc[h, :, cols]
            for level in range(FAR_LEVELS):
                weight = lw[h, NEAR_LEVELS + level, :, cols]
                weight = weight * (level_scale(NEAR_LEVELS + level) * SCALE)
                found += dot_nt(bk[level, rows, :], query) * weight
            mix[h, cols, :] = found.T.astype(BF16)
        for hop in (4, 3, 5, 2, 6, 1, 7):
            there = lax.rem(zed + hop, groups)
            pltpu.make_async_remote_copy(
                mix.at[h, pl.ds(pl.multiple_of(there * out_rows, out_rows), out_rows), :],
                tok.at[zed * heads + h],
                o_send.at[step],
                o_recv.at[step],
                device_id={"heads": there},
                device_id_type=MESH,
            ).start()
        tok[zed * heads + h] = mix[h, pl.ds(pl.multiple_of(zed * out_rows, out_rows), out_rows), :]

    @pl.when(zed < groups - 1)
    def _():
        pl.semaphore_wait(here_sem, groups - 1 - zed)

    def first(step, carry):
        far(step)
        return carry

    lax.fori_loop(0, heads // 2, first, 0)

    def second(step, carry):
        window(step)

        @pl.when(step == heads // 2)
        def _():
            for level in range(1, FAR_LEVELS):

                @pl.when(bit_of(level) == 1)
                def _():
                    piece = bk.at[level, other_half, :]
                    pltpu.make_async_copy(piece, piece, h_recv.at[level]).wait()

        far(step)
        return carry

    lax.fori_loop(heads // 2, heads, second, 0)

    lanes = jnp.zeros((out_rows, HEAD_DIM), F32)
    for step in range(heads):
        piece = tok.at[pl.ds(0, groups - 1)]
        pltpu.make_async_copy(piece, piece, o_recv.at[step]).wait()
        h = head_at(c, step)
        for group in range(groups):
            index = group * heads + h
            cols = pl.ds(pl.multiple_of(index * HEAD_DIM, HEAD_DIM), HEAD_DIM)
            gated = tok[index].astype(F32) * silu[:, cols]
            silu[:, cols] = gated
            lanes += gated * gated
    square = jnp.sum(lanes, axis=1, keepdims=True) * (1.0 / (groups * heads * HEAD_DIM))
    inverse = lax.rsqrt(square + EPSILON)
    for index in range(groups * heads):
        cols = pl.ds(index * HEAD_DIM, HEAD_DIM)
        out_ref[:, cols] = (gain_ref[:, cols] * silu[:, cols] * inverse).astype(BF16)

    piece = gat.at[pl.ds(0, row_n - 1)]
    pltpu.make_async_copy(piece, piece, a_send).wait()

    @pl.when(c == 0)
    def _():
        pltpu.make_async_copy(st, st, z_send).wait()

    for step in range(heads):
        pltpu.make_async_copy(k.at[0], k.at[0], ks_send.at[step]).wait()
        pltpu.make_async_copy(vt.at[0], vt.at[0], vs_send.at[step]).wait()
        piece = tok.at[pl.ds(0, groups - 1)]
        pltpu.make_async_copy(piece, piece, o_send.at[step]).wait()
    piece = tbuf.at[pl.ds(0, rows_x - 1)]
    pltpu.make_async_copy(piece, piece, t_send).wait()
    for level in range(1, FAR_LEVELS):
        if level <= low_levels:
            for own_bit in range(2):

                @pl.when(bit_of(level) == own_bit)
                def _():
                    piece = gat.at[pl.ds(0, rows_y // 2 - own_bit)]
                    pltpu.make_async_copy(piece, piece, c_send.at[level]).wait()

        else:

            @pl.when(bit_of(level) == 1)
            def _():
                piece = gat.at[pl.ds(0, rows_y - 1)]
                pltpu.make_async_copy(piece, piece, c_send.at[level]).wait()

        @pl.when(bit_of(level) == 1)
        def _():
            piece = bk.at[level, my_half, :]
            pltpu.make_async_copy(piece, piece, h_send.at[level]).wait()


def local(rows_x, rows_y, queries, key_vectors, values, level_weights, gate_branch, norm_gain):
    toks, width = queries.shape
    heads = width // HEAD_DIM
    groups = lax.axis_size("heads")
    out_rows, model = gate_branch.shape
    row_n = rows_y * 2
    part = heads * HEAD_DIM // row_n
    dma = pltpu.SemaphoreType.DMA
    hbm = pl.BlockSpec(memory_space=pl.ANY)
    vmem = pl.BlockSpec(memory_space=pltpu.VMEM)
    head_shape = (heads, toks, HEAD_DIM)
    turned_shape = (heads, HEAD_DIM, toks)
    return pl.pallas_call(
        functools.partial(kernel, rows_x, rows_y, groups),
        out_shape=jax.ShapeDtypeStruct((out_rows, model), BF16),
        in_specs=[hbm] * 6,
        out_specs=vmem,
        scratch_shapes=[
            pltpu.VMEM(head_shape, BF16),
            pltpu.VMEM(head_shape, BF16),
            pltpu.VMEM(head_shape, BF16),
            pltpu.VMEM(turned_shape, BF16),
            pltpu.VMEM(head_shape, BF16),
            pltpu.VMEM(turned_shape, BF16),
            pltpu.VMEM((heads, level_weights.shape[0], 1, toks), F32),
            pltpu.VMEM(gate_branch.shape, BF16),
            pltpu.VMEM(gate_branch.shape, F32),
            pltpu.VMEM(turned_shape, F32),
            pltpu.VMEM(head_shape, BF16),
            pltpu.VMEM((groups * heads, out_rows, HEAD_DIM), BF16),
            pltpu.VMEM((heads * HEAD_DIM, HEAD_DIM), BF16),
            pltpu.VMEM((row_n, part, HEAD_DIM), BF16),
            pltpu.VMEM((row_n // 2 - 1, part, HEAD_DIM), BF16),
            pltpu.VMEM((part, HEAD_DIM), F32),
            pltpu.VMEM((rows_x, part, HEAD_DIM), F32),
            pltpu.VMEM((2, part, HEAD_DIM), BF16),
            pltpu.VMEM((FAR_LEVELS, heads * HEAD_DIM, HEAD_DIM), BF16),
            pltpu.VMEM((1, model), F32),
            dma((heads,)),
            dma((heads,)),
            dma((heads,)),
            dma((heads,)),
            dma,
            dma,
            dma,
            dma,
            dma,
            dma,
            dma((heads,)),
            dma((heads,)),
            dma((heads,)),
            dma((heads,)),
            dma,
            dma,
            dma((FAR_LEVELS,)),
            dma((FAR_LEVELS,)),
            dma((FAR_LEVELS,)),
            dma((FAR_LEVELS,)),
            dma((heads,)),
            dma((heads,)),
            pltpu.SemaphoreType.REGULAR,
        ],
        compiler_params=pltpu.CompilerParams(
            collective_id=0, has_side_effects=True, vmem_limit_bytes=67043328
        ),
        name="layer",
    )(queries, key_vectors, values, level_weights, gate_branch, norm_gain.reshape(1, -1))


def solution(mesh):
    rows_x, rows_y = 4, 8
    return jax.shard_map(
        functools.partial(local, rows_x, rows_y),
        mesh=mesh,
        in_specs=(
            P("seq", "heads"),
            P("seq", "heads"),
            P("seq", "heads"),
            P(None, "heads", "seq"),
            P(("seq", "heads"), None),
            P(),
        ),
        out_specs=P(("seq", "heads"), None),
        check_vma=False,
    )
```

```python
import functools
import math

import jax
import jax.numpy as jnp
from jax import lax
from jax.experimental import pallas as pl
from jax.experimental.pallas import tpu as pltpu
from jax.sharding import PartitionSpec as P

HEAD_DIM = 128
EPSILON = 1e-06
NEAR_LEVELS = 10
FAR_LEVELS = 6
TILE = 128
MESH = pl.DeviceIdType.MESH
F32 = jnp.float32
BF16 = jnp.bfloat16
SCALE = HEAD_DIM**-0.5
NEG = -1e30


def level_scale(level):
    return 2.0 ** (-0.5 * max(level - 1, 0))


def dot_nt(a, b):
    return lax.dot_general(a, b, (((1,), (1,)), ((), ())), preferred_element_type=F32)


def dot_nn(a, b):
    return jnp.dot(a, b, preferred_element_type=F32)


def kernel(
    rows_x,
    rows_y,
    groups,
    q_hbm,
    k_hbm,
    v_hbm,
    lw_hbm,
    gate_hbm,
    gain_hbm,
    out_ref,
    q,
    k,
    v,
    vt,
    qn,
    past_out,
    past_in,
    stat_out,
    stat_in,
    own_acc,
    own_stat,
    lw,
    gate,
    silu,
    acc,
    mix,
    tok,
    st,
    gat,
    bsrc,
    tsrc,
    tbuf,
    xsrc,
    bk,
    gain_ref,
    q_sem,
    k_sem,
    v_sem,
    lw_sem,
    gate_sem,
    gain_sem,
    a_send,
    a_recv,
    z_send,
    z_recv,
    qs_send,
    qs_recv,
    ps_send,
    ps_recv,
    ss_send,
    ss_recv,
    t_send,
    t_recv,
    c_send,
    c_recv,
    h_send,
    h_recv,
    o_send,
    o_recv,
    here_sem,
):
    heads = k.shape[0]
    toks = k.shape[1]
    tiles = toks // TILE
    row_n = rows_y * 2
    seq_n = rows_x * row_n
    half = heads * HEAD_DIM // 2
    part = half // rows_y
    out_rows = toks // groups
    me = lax.axis_index("seq")
    zed = lax.axis_index("heads")
    x = me // row_n
    r = lax.rem(me, row_n)
    y = r // 2
    c = lax.rem(r, 2)

    def head_at(core, step):
        return lax.rem(core * (heads // 2) + step, heads)

    def row_id(place):
        return x * row_n + place

    barrier = pltpu.get_barrier_semaphore()
    greeted = (me > 0).astype(jnp.int32) + (me < seq_n - 1).astype(jnp.int32)
    for apart in (-1, 1):

        @pl.when((me + apart >= 0) & (me + apart < seq_n))
        def _():
            pl.semaphore_signal(
                barrier, inc=1, device_id={"seq": me + apart}, device_id_type=MESH
            )

    for step in range(1, row_n):
        pl.semaphore_signal(
            barrier,
            inc=1,
            device_id={"seq": row_id(lax.rem(r + step, row_n))},
            device_id_type=MESH,
        )
        greeted += 1
    for step in range(1, rows_x):
        pl.semaphore_signal(
            barrier,
            inc=1,
            device_id={"seq": lax.rem(x + step, rows_x) * row_n + r},
            device_id_type=MESH,
        )
        greeted += 1
    for step in range(1, groups):

        @pl.when(zed + step < groups)
        def _():
            pl.semaphore_signal(
                barrier, inc=1, device_id={"heads": zed + step}, device_id_type=MESH
            )


    for h in range(heads):
        cols = pl.ds(h * HEAD_DIM, HEAD_DIM)
        pltpu.make_async_copy(v_hbm.at[:, cols], v.at[h], v_sem.at[h]).start()
        pltpu.make_async_copy(k_hbm.at[:, cols], k.at[h], k_sem.at[h]).start()
    for h in range(heads):
        cols = pl.ds(h * HEAD_DIM, HEAD_DIM)
        pltpu.make_async_copy(q_hbm.at[:, cols], q.at[h], q_sem.at[h]).start()
    lw_copies = [
        pltpu.make_async_copy(lw_hbm.at[:, pl.ds(h, 1), :], lw.at[h], lw_sem.at[h])
        for h in range(heads)
    ]
    for copy in lw_copies:
        copy.start()
    gate_copy = pltpu.make_async_copy(gate_hbm, gate, gate_sem)
    gate_copy.start()
    gain_copy = pltpu.make_async_copy(gain_hbm, gain_ref, gain_sem)
    gain_copy.start()

    for h in range(heads):
        pltpu.make_async_copy(k_hbm.at[:, pl.ds(0, HEAD_DIM)], k.at[h], k_sem.at[h]).wait()
        pltpu.make_async_copy(v_hbm.at[:, pl.ds(0, HEAD_DIM)], v.at[h], v_sem.at[h]).wait()
        turned = v[h].T
        vt[h] = turned
        st[pl.ds(h * HEAD_DIM, HEAD_DIM), :] = dot_nn(turned, k[h]).astype(BF16)

    pl.semaphore_wait(barrier, greeted + zed)
    for step in range(1, groups):

        @pl.when(zed >= step)
        def _():
            pl.semaphore_signal(
                here_sem, inc=1, device_id={"heads": zed - step}, device_id_type=MESH
            )


    for step in sorted(range(1, row_n), key=lambda step: abs(step - row_n // 2)):
        place = lax.rem(r + step, row_n)
        rows = pl.multiple_of(lax.rem(place, 2) * half + (place // 2) * part, part)
        pltpu.make_async_remote_copy(
            st.at[pl.ds(rows, part), :],
            gat.at[r],
            a_send,
            a_recv,
            device_id={"seq": row_id(place)},
            device_id_type=MESH,
        ).start()
    mine = pl.multiple_of(c * half + y * part, part)
    gat[r] = st[pl.ds(mine, part), :]

    sibling = me + 1 - 2 * c

    @pl.when(c == 0)
    def _():
        pltpu.make_async_remote_copy(
            st, bk.at[0], z_send, z_recv, device_id={"seq": sibling}, device_id_type=MESH
        ).start()

    def send_queries(step):
        h = head_at(c, step)

        @pl.when(me > 0)
        def _():
            pltpu.make_async_remote_copy(
                q.at[h],
                qn.at[h],
                qs_send.at[step],
                qs_recv.at[step],
                device_id={"seq": me - 1},
                device_id_type=MESH,
            ).start()

    for h in range(heads):
        pltpu.make_async_copy(q_hbm.at[:, pl.ds(0, HEAD_DIM)], q.at[h], q_sem.at[h]).wait()
    for step in range(heads - 1):
        send_queries(step)

    @pl.when(me == 0)
    def _():
        past_in[...] = jnp.zeros(past_in.shape, BF16)
        stat_in[...] = jnp.full(stat_in.shape, NEG, F32)

    @pl.when(c == 0)
    def _():
        bk[0] = jnp.zeros(bk.shape[1:], BF16)

    def bit_of(level):
        return lax.rem(me // (1 << level), 2)

    for level in range(1, FAR_LEVELS):

        @pl.when(bit_of(level) == 0)
        def _():
            bk[level] = jnp.zeros(bk.shape[1:], BF16)

    gate_copy.wait()
    gain_copy.wait()
    wide = gate[...].astype(F32)
    silu[...] = wide * jax.nn.sigmoid(wide)

    for copy in lw_copies:
        copy.wait()
    key_at = lax.broadcasted_iota(jnp.int32, (TILE, TILE), 0)
    query_at = lax.broadcasted_iota(jnp.int32, (TILE, TILE), 1)
    gain_exp = SCALE * math.log2(math.e)

    def within(step, carry):
        h = head_at(c, step)
        causal = key_at <= query_at
        apart = key_at ^ query_at
        for i in range(tiles):
            cols = pl.ds(i * TILE, TILE)
            scores = dot_nt(k[h, pl.ds(0, (i + 1) * TILE), :], q[h, cols, :])
            parts = [scores[j * TILE : (j + 1) * TILE] for j in range(i + 1)]
            seen = parts[:-1] + [jnp.where(causal, parts[-1], NEG)]
            top = functools.reduce(jnp.maximum, seen)
            top = jnp.max(top, axis=0, keepdims=True) * gain_exp
            powers = [jnp.exp2(tile * gain_exp - top) for tile in seen]
            mass = jnp.sum(functools.reduce(jnp.add, powers), axis=0, keepdims=True)
            rows = [
                lw[h, level, :, cols] * (level_scale(level) * SCALE) for level in range(NEAR_LEVELS)
            ]
            near = [
                parts[j] * rows[TILE.bit_length() - 1 + (i ^ j).bit_length()] for j in range(i)
            ]
            mixed = jnp.broadcast_to(rows[0], (TILE, TILE))
            for level in range(1, TILE.bit_length()):
                mixed = jnp.where(apart >= 1 << (level - 1), rows[level], mixed)
            near.append(jnp.where(causal, parts[i] * mixed, 0.0))
            both = jnp.concatenate(
                [
                    jnp.concatenate([tile.astype(BF16) for tile in powers], axis=0),
                    jnp.concatenate([tile.astype(BF16) for tile in near], axis=0),
                ],
                axis=1,
            )
            found = dot_nn(vt[h, :, pl.ds(0, (i + 1) * TILE)], both)
            own_acc[h, :, cols] = found[:, :TILE]
            acc[h, :, cols] = found[:, TILE:]
            own_stat[h, 0:1, cols] = top
            own_stat[h, 1:2, cols] = mass
        return carry

    lax.fori_loop(0, heads, within, 0)

    pltpu.make_async_copy(
        gat.at[pl.ds(0, row_n - 1)], gat.at[pl.ds(0, row_n - 1)], a_recv
    ).wait()
    sums = [gat[i].astype(F32) for i in range(row_n)]
    level_sums = []
    while len(sums) > 1:
        sums = [sums[2 * i] + sums[2 * i + 1] for i in range(len(sums) // 2)]
        level_sums.append(sums)
    low_levels = len(level_sums) - 1
    firsts = []
    count = 0
    for level_list in level_sums[:-1]:
        firsts.append(count)
        for i in range(0, len(level_list), 2):
            bsrc[count] = level_list[i].astype(BF16)
            count += 1
    total = level_sums[-1][0]
    tsrc[...] = total
    tbuf[x] = total
    for step in range(1, rows_x):
        pltpu.make_async_remote_copy(
            tsrc,
            tbuf.at[x],
            t_send,
            t_recv,
            device_id={"seq": lax.rem(x + step, rows_x) * row_n + r},
            device_id_type=MESH,
        ).start()
    for level in range(low_levels, 0, -1):
        for step in (4, 3, 5, 2, 6, 1, 7, 0):
            place = lax.rem(y + step, rows_y)
            src = bsrc.at[firsts[level - 1] + place // (1 << level)]
            dst = bk.at[level, pl.ds(mine, part), :]

            @pl.when(lax.rem(place // (1 << (level - 1)), 2) == 1)
            def _():
                if step == 0:
                    pltpu.make_async_copy(src, dst, c_recv.at[level]).start()
                else:
                    pltpu.make_async_remote_copy(
                        src,
                        dst,
                        c_send.at[level],
                        c_recv.at[level],
                        device_id={"seq": row_id(place * 2 + c)},
                        device_id_type=MESH,
                    ).start()

    send_queries(heads - 1)

    def onward(step, carry):
        h = head_at(1 - c, step)
        pltpu.make_async_copy(q.at[h], qn.at[h], qs_recv.at[step]).wait()
        later = key_at > query_at
        for i in range(tiles):
            cols = pl.ds(i * TILE, TILE)
            count = tiles - i
            scores = dot_nt(k[h, pl.ds(i * TILE, count * TILE), :], qn[h, cols, :])
            parts = [scores[j * TILE : (j + 1) * TILE] for j in range(count)]
            seen = [jnp.where(later, parts[0], NEG)] + parts[1:]
            top = functools.reduce(jnp.maximum, seen)
            top = jnp.max(top, axis=0, keepdims=True) * gain_exp
            powers = [jnp.exp2(tile * gain_exp - top) for tile in seen]
            powers[0] = jnp.where(later, powers[0], 0.0)
            mass = jnp.sum(functools.reduce(jnp.add, powers), axis=0, keepdims=True)
            both = jnp.concatenate([tile.astype(BF16) for tile in powers], axis=0)
            found = dot_nn(vt[h, :, pl.ds(i * TILE, count * TILE)], both)
            past_out[h, :, cols] = found.astype(BF16)
            stat_out[h, 0:1, cols] = top
            stat_out[h, 1:2, cols] = mass
        for src, dst, send, recv in (
            (past_out, past_in, ps_send, ps_recv),
            (stat_out, stat_in, ss_send, ss_recv),
        ):
            pltpu.make_async_remote_copy(
                src.at[h],
                dst.at[h],
                send.at[step],
                recv.at[step],
                device_id={"seq": me + 1},
                device_id_type=MESH,
            ).start()
        return carry

    pltpu.make_async_copy(
        tbuf.at[pl.ds(0, rows_x - 1)], tbuf.at[pl.ds(0, rows_x - 1)], t_recv
    ).wait()
    xsrc[0] = tbuf[lax.max(x - 1, 0)].astype(BF16)
    xsrc[1] = (tbuf[0] + tbuf[1]).astype(BF16)
    for up in range(FAR_LEVELS - 1 - low_levels):
        level = low_levels + 1 + up

        @pl.when(bit_of(level) == 1)
        def _():
            for step in (4, 3, 5, 2, 6, 1, 7, 0):
                place = lax.rem(y + step, rows_y)
                src = xsrc.at[up]
                dst = bk.at[level, pl.ds(mine, part), :]
                if step == 0:
                    pltpu.make_async_copy(src, dst, c_recv.at[level]).start()
                else:
                    pltpu.make_async_remote_copy(
                        src,
                        dst,
                        c_send.at[level],
                        c_recv.at[level],
                        device_id={"seq": row_id(place * 2 + c)},
                        device_id_type=MESH,
                    ).start()

    @pl.when(me < seq_n - 1)
    def _():
        lax.fori_loop(0, heads, onward, 0)


    my_half = pl.ds(pl.multiple_of(c * half, half), half)
    other_half = pl.ds(pl.multiple_of((1 - c) * half, half), half)

    def take(level):
        @pl.when(bit_of(level) == 1)
        def _():
            piece = bk.at[level, my_half, :]
            pltpu.make_async_copy(piece, piece, c_recv.at[level]).wait()
            pltpu.make_async_remote_copy(
                piece,
                piece,
                h_send.at[level],
                h_recv.at[level],
                device_id={"seq": sibling},
                device_id_type=MESH,
            ).start()

    def take_other(level):
        @pl.when(bit_of(level) == 1)
        def _():
            piece = bk.at[level, other_half, :]
            pltpu.make_async_copy(piece, piece, h_recv.at[level]).wait()

    wide_cols = min(2 * TILE, toks)

    def far(h, cols, levels, found):
        rows = pl.ds(pl.multiple_of(h * HEAD_DIM, HEAD_DIM), HEAD_DIM)
        query = q[h, cols, :]
        for level in levels:
            weight = lw[h, NEAR_LEVELS + level, :, cols]
            weight = weight * (level_scale(NEAR_LEVELS + level) * SCALE)
            found += dot_nt(bk[level, rows, :], query) * weight
        return found

    def finish(step, carry):
        h = head_at(c, step)

        @pl.when(me > 0)
        def _():
            pltpu.make_async_copy(vt.at[h], past_in.at[h], ps_recv.at[step]).wait()
            pltpu.make_async_copy(stat_out.at[h], stat_in.at[h], ss_recv.at[step]).wait()

        for start in range(0, toks, wide_cols):
            cols = pl.ds(start, wide_cols)
            own_top = own_stat[h, 0:1, cols]
            past_top = stat_in[h, 0:1, cols]
            top = jnp.maximum(own_top, past_top)
            own_part = jnp.exp2(own_top - top)
            past_part = jnp.exp2(past_top - top)
            share = 1.0 / (own_part * own_stat[h, 1:2, cols] + past_part * stat_in[h, 1:2, cols])
            found = acc[h, :, cols] + own_acc[h, :, cols] * (own_part * share)
            found += past_in[h, :, cols].astype(F32) * (past_part * share)
            found = far(h, cols, range(FAR_LEVELS), found)
            mix[h, cols, :] = found.T.astype(BF16)
        for there in range(groups):

            @pl.when(zed != there)
            def _():
                pltpu.make_async_remote_copy(
                    mix.at[h, pl.ds(there * out_rows, out_rows), :],
                    tok.at[zed, h],
                    o_send.at[step],
                    o_recv.at[step],
                    device_id={"heads": there},
                    device_id_type=MESH,
                ).start()

        tok[zed, h] = mix[h, pl.ds(pl.multiple_of(zed * out_rows, out_rows), out_rows), :]
        return carry

    for level in range(1, FAR_LEVELS):
        take(level)

    @pl.when(c == 1)
    def _():
        pltpu.make_async_copy(st, bk.at[0], z_recv).wait()

    @pl.when(zed < groups - 1)
    def _():
        pl.semaphore_wait(here_sem, groups - 1 - zed)

    lax.fori_loop(0, heads // 2, finish, 0)
    for level in range(1, FAR_LEVELS):
        take_other(level)
    lax.fori_loop(heads // 2, heads, finish, 0)

    lanes = jnp.zeros((out_rows, HEAD_DIM), F32)
    for step in range(heads):
        piece = tok.at[0:groups - 1, 0]
        pltpu.make_async_copy(piece, piece, o_recv.at[step]).wait()
        h = head_at(c, step)
        for group in range(groups):
            cols = pl.ds(pl.multiple_of((group * heads + h) * HEAD_DIM, HEAD_DIM), HEAD_DIM)
            gated = tok[group, h].astype(F32) * silu[:, cols]
            silu[:, cols] = gated
            lanes += gated * gated
    square = jnp.sum(lanes, axis=1, keepdims=True) * (1.0 / (groups * heads * HEAD_DIM))
    inverse = lax.rsqrt(square + EPSILON)
    for index in range(groups * heads):
        cols = pl.ds(index * HEAD_DIM, HEAD_DIM)
        out_ref[:, cols] = (gain_ref[:, cols] * silu[:, cols] * inverse).astype(BF16)

    piece = gat.at[pl.ds(0, row_n - 1)]
    pltpu.make_async_copy(piece, piece, a_send).wait()

    @pl.when(c == 0)
    def _():
        pltpu.make_async_copy(st, st, z_send).wait()

    for step in range(heads):

        @pl.when(me > 0)
        def _():
            pltpu.make_async_copy(q.at[0], q.at[0], qs_send.at[step]).wait()

        @pl.when(me < seq_n - 1)
        def _():
            pltpu.make_async_copy(vt.at[0], vt.at[0], ps_send.at[step]).wait()
            pltpu.make_async_copy(stat_out.at[0], stat_out.at[0], ss_send.at[step]).wait()

        piece = tok.at[0 : groups - 1, 0]
        pltpu.make_async_copy(piece, piece, o_send.at[step]).wait()
    piece = tbuf.at[pl.ds(0, rows_x - 1)]
    pltpu.make_async_copy(piece, piece, t_send).wait()
    for level in range(1, FAR_LEVELS):
        if level <= low_levels:
            for own_bit in range(2):

                @pl.when(bit_of(level) == own_bit)
                def _():
                    piece = gat.at[pl.ds(0, rows_y // 2 - own_bit)]
                    pltpu.make_async_copy(piece, piece, c_send.at[level]).wait()

        else:

            @pl.when(bit_of(level) == 1)
            def _():
                piece = gat.at[pl.ds(0, rows_y - 1)]
                pltpu.make_async_copy(piece, piece, c_send.at[level]).wait()

        @pl.when(bit_of(level) == 1)
        def _():
            piece = bk.at[level, my_half, :]
            pltpu.make_async_copy(piece, piece, h_send.at[level]).wait()


def local(rows_x, rows_y, queries, key_vectors, values, level_weights, gate_branch, norm_gain):
    toks, width = queries.shape
    heads = width // HEAD_DIM
    groups = lax.axis_size("heads")
    out_rows, model = gate_branch.shape
    row_n = rows_y * 2
    part = heads * HEAD_DIM // row_n
    arrays = [queries, key_vectors, values, level_weights, gate_branch, norm_gain.reshape(1, -1)]
    dma = pltpu.SemaphoreType.DMA
    hbm = pl.BlockSpec(memory_space=pl.ANY)
    vmem = pl.BlockSpec(memory_space=pltpu.VMEM)
    head_shape = (heads, toks, HEAD_DIM)
    turned_shape = (heads, HEAD_DIM, toks)
    return pl.pallas_call(
        functools.partial(kernel, rows_x, rows_y, groups),
        out_shape=jax.ShapeDtypeStruct((out_rows, model), BF16),
        in_specs=[hbm] * 6,
        out_specs=vmem,
        scratch_shapes=[
            pltpu.VMEM(head_shape, BF16),
            pltpu.VMEM(head_shape, BF16),
            pltpu.VMEM(head_shape, BF16),
            pltpu.VMEM(turned_shape, BF16),
            pltpu.VMEM(head_shape, BF16),
            pltpu.VMEM(turned_shape, BF16),
            pltpu.VMEM(turned_shape, BF16),
            pltpu.VMEM((heads, 2, toks), F32),
            pltpu.VMEM((heads, 2, toks), F32),
            pltpu.VMEM(turned_shape, F32),
            pltpu.VMEM((heads, 2, toks), F32),
            pltpu.VMEM((heads, level_weights.shape[0], 1, toks), F32),
            pltpu.VMEM(gate_branch.shape, BF16),
            pltpu.VMEM(gate_branch.shape, F32),
            pltpu.VMEM(turned_shape, F32),
            pltpu.VMEM(head_shape, BF16),
            pltpu.VMEM((groups, heads, out_rows, HEAD_DIM), BF16),
            pltpu.VMEM((heads * HEAD_DIM, HEAD_DIM), BF16),
            pltpu.VMEM((row_n, part, HEAD_DIM), BF16),
            pltpu.VMEM((row_n // 2 - 1, part, HEAD_DIM), BF16),
            pltpu.VMEM((part, HEAD_DIM), F32),
            pltpu.VMEM((rows_x, part, HEAD_DIM), F32),
            pltpu.VMEM((2, part, HEAD_DIM), BF16),
            pltpu.VMEM((FAR_LEVELS, heads * HEAD_DIM, HEAD_DIM), BF16),
            pltpu.VMEM((1, model), F32),
            dma((heads,)),
            dma((heads,)),
            dma((heads,)),
            dma((heads,)),
            dma,
            dma,
            dma,
            dma,
            dma,
            dma,
            dma((heads,)),
            dma((heads,)),
            dma((heads,)),
            dma((heads,)),
            dma((heads,)),
            dma((heads,)),
            dma,
            dma,
            dma((FAR_LEVELS,)),
            dma((FAR_LEVELS,)),
            dma((FAR_LEVELS,)),
            dma((FAR_LEVELS,)),
            dma((heads,)),
            dma((heads,)),
            pltpu.SemaphoreType.REGULAR,
        ],
        compiler_params=pltpu.CompilerParams(
            collective_id=0, has_side_effects=True, vmem_limit_bytes=24 << 20
        ),
        name="layer",
    )(*[pltpu.with_memory_space_constraint(array, pltpu.HBM) for array in arrays])


def solution(mesh):
    rows_x, rows_y = 4, 8
    return jax.shard_map(
        functools.partial(local, rows_x, rows_y),
        mesh=mesh,
        in_specs=(
            P("seq", "heads"),
            P("seq", "heads"),
            P("seq", "heads"),
            P(None, "heads", "seq"),
            P(("seq", "heads"), None),
            P(),
        ),
        out_specs=P(("seq", "heads"), None),
        check_vma=False,
    )
```

```python
import functools
import math

import jax
import jax.numpy as jnp
from jax import lax
from jax.experimental import pallas as pl
from jax.experimental.pallas import tpu as pltpu
from jax.sharding import PartitionSpec as P

HEAD_DIM = 128
EPSILON = 1e-06
NEAR_LEVELS = 10
FAR_LEVELS = 6
TILE = 128
MESH = pl.DeviceIdType.MESH
F32 = jnp.float32
BF16 = jnp.bfloat16
SCALE = HEAD_DIM**-0.5
NEG = -1e30


def level_scale(level):
    return 2.0 ** (-0.5 * max(level - 1, 0))


def dot_nt(a, b):
    return lax.dot_general(a, b, (((1,), (1,)), ((), ())), preferred_element_type=F32)


def dot_nn(a, b):
    return jnp.dot(a, b, preferred_element_type=F32)


def kernel(
    rows_x,
    rows_y,
    groups,
    q_hbm,
    k_hbm,
    v_hbm,
    lw_hbm,
    gate_hbm,
    gain_hbm,
    out_ref,
    q,
    k,
    v,
    vt,
    qn,
    past_out,
    past_in,
    stat_out,
    stat_in,
    own_acc,
    own_stat,
    lw,
    gate,
    silu,
    acc,
    mix,
    tok,
    st,
    sib,
    chip,
    gat,
    bsrc,
    tsrc,
    tbuf,
    xsrc,
    bk,
    gain_ref,
    q_sem,
    k_sem,
    v_sem,
    lw_sem,
    gate_sem,
    gain_sem,
    s_send,
    s_recv,
    a_send,
    a_recv,
    z_send,
    z_recv,
    qs_send,
    qs_recv,
    ps_send,
    ps_recv,
    ss_send,
    ss_recv,
    t_send,
    t_recv,
    c_send,
    c_recv,
    h_send,
    h_recv,
    o_send,
    o_recv,
    here_sem,
):
    heads = k.shape[0]
    toks = k.shape[1]
    tiles = toks // TILE
    row_n = rows_y * 2
    seq_n = rows_x * row_n
    half = heads * HEAD_DIM // 2
    part = half // rows_y
    out_rows = toks // groups
    me = lax.axis_index("seq")
    zed = lax.axis_index("heads")
    x = me // row_n
    r = lax.rem(me, row_n)
    y = r // 2
    c = lax.rem(r, 2)

    def head_at(core, step):
        return lax.rem(core * (heads // 2) + step, heads)

    def bit_of(level):
        return lax.rem(me // (1 << level), 2)

    def row_id(place):
        return x * row_n + place

    barrier = pltpu.get_barrier_semaphore()
    greeted = (me > 0).astype(jnp.int32) + (me < seq_n - 1).astype(jnp.int32)
    for apart in (-1, 1):

        @pl.when((me + apart >= 0) & (me + apart < seq_n))
        def _():
            pl.semaphore_signal(
                barrier, inc=1, device_id={"seq": me + apart}, device_id_type=MESH
            )

    for step in (4, 3, 5, 2, 6, 1, 7):
        pl.semaphore_signal(
            barrier,
            inc=1,
            device_id={"seq": row_id(lax.rem(y + step, rows_y) * 2 + c)},
            device_id_type=MESH,
        )
        greeted += 1
    for step in range(1, rows_x):
        pl.semaphore_signal(
            barrier,
            inc=1,
            device_id={"seq": lax.rem(x + step, rows_x) * row_n + r},
            device_id_type=MESH,
        )
        greeted += 1
    for step in range(1, groups):

        @pl.when(zed + step < groups)
        def _():
            pl.semaphore_signal(
                barrier, inc=1, device_id={"heads": zed + step}, device_id_type=MESH
            )


    for h in range(heads):
        cols = pl.ds(h * HEAD_DIM, HEAD_DIM)
        pltpu.make_async_copy(v_hbm.at[:, cols], v.at[h], v_sem.at[h]).start()
        pltpu.make_async_copy(k_hbm.at[:, cols], k.at[h], k_sem.at[h]).start()
    for h in range(heads):
        cols = pl.ds(h * HEAD_DIM, HEAD_DIM)
        pltpu.make_async_copy(q_hbm.at[:, cols], q.at[h], q_sem.at[h]).start()
    lw_copies = [
        pltpu.make_async_copy(lw_hbm.at[:, pl.ds(h, 1), :], lw.at[h], lw_sem.at[h])
        for h in range(heads)
    ]
    for copy in lw_copies:
        copy.start()
    gate_copy = pltpu.make_async_copy(gate_hbm, gate, gate_sem)
    gate_copy.start()
    gain_copy = pltpu.make_async_copy(gain_hbm, gain_ref, gain_sem)
    gain_copy.start()

    for h in range(heads):
        pltpu.make_async_copy(k_hbm.at[:, pl.ds(0, HEAD_DIM)], k.at[h], k_sem.at[h]).wait()
        pltpu.make_async_copy(v_hbm.at[:, pl.ds(0, HEAD_DIM)], v.at[h], v_sem.at[h]).wait()
        st[pl.ds(h * HEAD_DIM, HEAD_DIM), :] = lax.dot_general(
            v[h], k[h], (((0,), (0,)), ((), ())), preferred_element_type=F32
        ).astype(BF16)

    pl.semaphore_wait(barrier, greeted + zed)
    for step in range(1, groups):

        @pl.when(zed >= step)
        def _():
            pl.semaphore_signal(
                here_sem, inc=1, device_id={"heads": zed - step}, device_id_type=MESH
            )


    sibling = me + 1 - 2 * c
    mine = pl.multiple_of(c * half + y * part, part)
    my_half = pl.ds(pl.multiple_of(c * half, half), half)
    other_half = pl.ds(pl.multiple_of((1 - c) * half, half), half)
    pltpu.make_async_remote_copy(
        st.at[other_half, :], sib, s_send, s_recv, device_id={"seq": sibling}, device_id_type=MESH
    ).start()

    def send_queries(step):
        h = head_at(c, step)

        @pl.when(me > 0)
        def _():
            pltpu.make_async_remote_copy(
                q.at[h],
                qn.at[h],
                qs_send.at[step],
                qs_recv.at[step],
                device_id={"seq": me - 1},
                device_id_type=MESH,
            ).start()

    for h in range(heads):
        pltpu.make_async_copy(q_hbm.at[:, pl.ds(0, HEAD_DIM)], q.at[h], q_sem.at[h]).wait()
    send_queries(0)

    @pl.when(c == 0)
    def _():
        pltpu.make_async_remote_copy(
            st, bk.at[0], z_send, z_recv, device_id={"seq": sibling}, device_id_type=MESH
        ).start()

    @pl.when(me == 0)
    def _():
        past_in[...] = jnp.zeros(past_in.shape, BF16)
        stat_in[...] = jnp.full(stat_in.shape, NEG, F32)

    @pl.when(c == 0)
    def _():
        bk[0] = jnp.zeros(bk.shape[1:], BF16)

    for level in range(1, FAR_LEVELS):

        @pl.when(bit_of(level) == 0)
        def _():
            bk[level] = jnp.zeros(bk.shape[1:], BF16)

    gate_copy.wait()
    gain_copy.wait()
    wide = gate[...].astype(F32)
    silu[...] = wide * jax.nn.sigmoid(wide)

    pltpu.make_async_copy(sib, sib, s_recv).wait()
    chip[...] = (st[my_half, :].astype(F32) + sib[...].astype(F32)).astype(BF16)
    for step in (4, 3, 5, 2, 6, 1, 7):
        place = lax.rem(y + step, rows_y)
        pltpu.make_async_remote_copy(
            chip.at[pl.ds(pl.multiple_of(place * part, part), part), :],
            gat.at[y],
            a_send,
            a_recv,
            device_id={"seq": row_id(place * 2 + c)},
            device_id_type=MESH,
        ).start()

    @pl.when(bit_of(1) == 0)
    def _():
        pltpu.make_async_remote_copy(
            chip,
            bk.at[1, my_half, :],
            c_send.at[1],
            c_recv.at[1],
            device_id={"seq": me + 2},
            device_id_type=MESH,
        ).start()

    gat[y] = chip[pl.ds(pl.multiple_of(y * part, part), part), :]
    send_queries(1)

    for copy in lw_copies:
        copy.wait()
    key_at = lax.broadcasted_iota(jnp.int32, (TILE, TILE), 0)
    query_at = lax.broadcasted_iota(jnp.int32, (TILE, TILE), 1)
    gain_exp = SCALE * math.log2(math.e)

    def within(step, carry):
        h = head_at(c, step)
        vt[h] = v[h].T
        causal = key_at <= query_at
        apart = key_at ^ query_at
        for i in range(tiles):
            cols = pl.ds(i * TILE, TILE)
            scores = dot_nt(k[h, pl.ds(0, (i + 1) * TILE), :], q[h, cols, :])
            parts = [scores[j * TILE : (j + 1) * TILE] for j in range(i + 1)]
            seen = parts[:-1] + [jnp.where(causal, parts[-1], NEG)]
            top = functools.reduce(jnp.maximum, seen)
            top = jnp.max(top, axis=0, keepdims=True) * gain_exp
            powers = [jnp.exp2(tile * gain_exp - top) for tile in seen]
            mass = jnp.sum(functools.reduce(jnp.add, powers), axis=0, keepdims=True)
            rows = [
                lw[h, level, :, cols] * (level_scale(level) * SCALE) for level in range(NEAR_LEVELS)
            ]
            near = [
                parts[j] * rows[TILE.bit_length() - 1 + (i ^ j).bit_length()] for j in range(i)
            ]
            mixed = jnp.broadcast_to(rows[0], (TILE, TILE))
            for level in range(1, TILE.bit_length()):
                mixed = jnp.where(apart >= 1 << (level - 1), rows[level], mixed)
            near.append(jnp.where(causal, parts[i] * mixed, 0.0))
            both = jnp.concatenate(
                [
                    jnp.concatenate([tile.astype(BF16) for tile in powers], axis=0),
                    jnp.concatenate([tile.astype(BF16) for tile in near], axis=0),
                ],
                axis=1,
            )
            found = dot_nn(vt[h, :, pl.ds(0, (i + 1) * TILE)], both)
            own_acc[h, :, cols] = found[:, :TILE]
            acc[h, :, cols] = found[:, TILE:]
            own_stat[h, 0:1, cols] = top
            own_stat[h, 1:2, cols] = mass
        return carry

    lax.fori_loop(0, heads, within, 0)

    def onward(step, carry):
        h = head_at(1 - c, step)
        pltpu.make_async_copy(q.at[h], qn.at[h], qs_recv.at[step]).wait()
        later = key_at > query_at
        for i in range(tiles):
            cols = pl.ds(i * TILE, TILE)
            count = tiles - i
            scores = dot_nt(k[h, pl.ds(i * TILE, count * TILE), :], qn[h, cols, :])
            parts = [scores[j * TILE : (j + 1) * TILE] for j in range(count)]
            seen = [jnp.where(later, parts[0], NEG)] + parts[1:]
            top = functools.reduce(jnp.maximum, seen)
            top = jnp.max(top, axis=0, keepdims=True) * gain_exp
            powers = [jnp.exp2(tile * gain_exp - top) for tile in seen]
            powers[0] = jnp.where(later, powers[0], 0.0)
            mass = jnp.sum(functools.reduce(jnp.add, powers), axis=0, keepdims=True)
            both = jnp.concatenate([tile.astype(BF16) for tile in powers], axis=0)
            found = dot_nn(vt[h, :, pl.ds(i * TILE, count * TILE)], both)
            past_out[h, :, cols] = found.astype(BF16)
            stat_out[h, 0:1, cols] = top
            stat_out[h, 1:2, cols] = mass
        for src, dst, send, recv in (
            (past_out, past_in, ps_send, ps_recv),
            (stat_out, stat_in, ss_send, ss_recv),
        ):
            pltpu.make_async_remote_copy(
                src.at[h],
                dst.at[h],
                send.at[step],
                recv.at[step],
                device_id={"seq": me + 1},
                device_id_type=MESH,
            ).start()
        return carry

    @pl.when(me < seq_n - 1)
    def _():
        onward(0, 0)

    pltpu.make_async_copy(
        gat.at[pl.ds(0, rows_y - 1)], gat.at[pl.ds(0, rows_y - 1)], a_recv
    ).wait()
    sums = [gat[i].astype(F32) for i in range(rows_y)]
    level_sums = []
    while len(sums) > 1:
        sums = [sums[2 * i] + sums[2 * i + 1] for i in range(len(sums) // 2)]
        level_sums.append(sums)
    low_levels = len(level_sums)
    firsts = {}
    count = 0
    for level, level_list in enumerate(level_sums[:-1], 2):
        firsts[level] = count
        for i in range(0, len(level_list), 2):
            bsrc[count] = level_list[i].astype(BF16)
            count += 1
    total = level_sums[-1][0]
    tsrc[...] = total
    tbuf[x] = total
    for step in range(1, rows_x):
        pltpu.make_async_remote_copy(
            tsrc,
            tbuf.at[x],
            t_send,
            t_recv,
            device_id={"seq": lax.rem(x + step, rows_x) * row_n + r},
            device_id_type=MESH,
        ).start()
    for level in range(low_levels, 1, -1):
        for step in (4, 3, 5, 2, 6, 1, 7, 0):
            place = lax.rem(y + step, rows_y)
            src = bsrc.at[firsts[level] + place // (1 << level)]
            dst = bk.at[level, pl.ds(mine, part), :]

            @pl.when(lax.rem(place // (1 << (level - 1)), 2) == 1)
            def _():
                if step == 0:
                    pltpu.make_async_copy(src, dst, c_recv.at[level]).start()
                else:
                    pltpu.make_async_remote_copy(
                        src,
                        dst,
                        c_send.at[level],
                        c_recv.at[level],
                        device_id={"seq": row_id(place * 2 + c)},
                        device_id_type=MESH,
                    ).start()

    send_queries(2)

    pltpu.make_async_copy(
        tbuf.at[pl.ds(0, rows_x - 1)], tbuf.at[pl.ds(0, rows_x - 1)], t_recv
    ).wait()
    xsrc[0] = tbuf[lax.max(x - 1, 0)].astype(BF16)
    xsrc[1] = (tbuf[0] + tbuf[1]).astype(BF16)
    for up in range(FAR_LEVELS - 1 - low_levels):
        level = low_levels + 1 + up

        @pl.when(bit_of(level) == 1)
        def _():
            for step in (4, 3, 5, 2, 6, 1, 7, 0):
                place = lax.rem(y + step, rows_y)
                src = xsrc.at[up]
                dst = bk.at[level, pl.ds(mine, part), :]
                if step == 0:
                    pltpu.make_async_copy(src, dst, c_recv.at[level]).start()
                else:
                    pltpu.make_async_remote_copy(
                        src,
                        dst,
                        c_send.at[level],
                        c_recv.at[level],
                        device_id={"seq": row_id(place * 2 + c)},
                        device_id_type=MESH,
                    ).start()

    send_queries(3)

    @pl.when(me < seq_n - 1)
    def _():
        lax.fori_loop(1, heads - 1, onward, 0)

    def take(level):
        @pl.when(bit_of(level) == 1)
        def _():
            piece = bk.at[level, my_half, :]
            pltpu.make_async_copy(piece, piece, c_recv.at[level]).wait()
            pltpu.make_async_remote_copy(
                piece,
                piece,
                h_send.at[level],
                h_recv.at[level],
                device_id={"seq": sibling},
                device_id_type=MESH,
            ).start()

    def take_other(level):
        @pl.when(bit_of(level) == 1)
        def _():
            piece = bk.at[level, other_half, :]
            pltpu.make_async_copy(piece, piece, h_recv.at[level]).wait()

    wide_cols = min(2 * TILE, toks)

    def far(h, cols, levels, found):
        rows = pl.ds(pl.multiple_of(h * HEAD_DIM, HEAD_DIM), HEAD_DIM)
        query = q[h, cols, :]
        for level in levels:
            weight = lw[h, NEAR_LEVELS + level, :, cols]
            weight = weight * (level_scale(NEAR_LEVELS + level) * SCALE)
            found += dot_nt(bk[level, rows, :], query) * weight
        return found

    def finish(step, carry):
        h = head_at(c, step)

        @pl.when(me > 0)
        def _():
            pltpu.make_async_copy(vt.at[h], past_in.at[h], ps_recv.at[step]).wait()
            pltpu.make_async_copy(stat_out.at[h], stat_in.at[h], ss_recv.at[step]).wait()

        for start in range(0, toks, wide_cols):
            cols = pl.ds(start, wide_cols)
            own_top = own_stat[h, 0:1, cols]
            past_top = stat_in[h, 0:1, cols]
            top = jnp.maximum(own_top, past_top)
            own_part = jnp.exp2(own_top - top)
            past_part = jnp.exp2(past_top - top)
            share = 1.0 / (own_part * own_stat[h, 1:2, cols] + past_part * stat_in[h, 1:2, cols])
            found = acc[h, :, cols] + own_acc[h, :, cols] * (own_part * share)
            found += past_in[h, :, cols].astype(F32) * (past_part * share)
            found = far(h, cols, range(FAR_LEVELS), found)
            mix[h, cols, :] = found.T.astype(BF16)
        for there in range(groups):

            @pl.when(zed != there)
            def _():
                pltpu.make_async_remote_copy(
                    mix.at[h, pl.ds(there * out_rows, out_rows), :],
                    tok.at[zed, h],
                    o_send.at[step],
                    o_recv.at[step],
                    device_id={"heads": there},
                    device_id_type=MESH,
                ).start()

        tok[zed, h] = mix[h, pl.ds(pl.multiple_of(zed * out_rows, out_rows), out_rows), :]
        return carry

    for level in range(1, FAR_LEVELS):
        take(level)

    @pl.when(c == 1)
    def _():
        pltpu.make_async_copy(st, bk.at[0], z_recv).wait()

    @pl.when(zed < groups - 1)
    def _():
        pl.semaphore_wait(here_sem, groups - 1 - zed)

    lax.fori_loop(0, heads // 2, finish, 0)

    @pl.when(me < seq_n - 1)
    def _():
        onward(heads - 1, 0)

    for level in range(1, FAR_LEVELS):
        take_other(level)
    lax.fori_loop(heads // 2, heads, finish, 0)

    lanes = jnp.zeros((out_rows, HEAD_DIM), F32)
    for step in range(heads):
        piece = tok.at[0:groups - 1, 0]
        pltpu.make_async_copy(piece, piece, o_recv.at[step]).wait()
        h = head_at(c, step)
        for group in range(groups):
            cols = pl.ds(pl.multiple_of((group * heads + h) * HEAD_DIM, HEAD_DIM), HEAD_DIM)
            gated = tok[group, h].astype(F32) * silu[:, cols]
            silu[:, cols] = gated
            lanes += gated * gated
    square = jnp.sum(lanes, axis=1, keepdims=True) * (1.0 / (groups * heads * HEAD_DIM))
    inverse = lax.rsqrt(square + EPSILON)
    for index in range(groups * heads):
        cols = pl.ds(index * HEAD_DIM, HEAD_DIM)
        out_ref[:, cols] = (gain_ref[:, cols] * silu[:, cols] * inverse).astype(BF16)

    piece = gat.at[pl.ds(0, rows_y - 1)]
    pltpu.make_async_copy(piece, piece, a_send).wait()
    pltpu.make_async_copy(sib, sib, s_send).wait()

    @pl.when(c == 0)
    def _():
        pltpu.make_async_copy(st, st, z_send).wait()

    for step in range(heads):

        @pl.when(me > 0)
        def _():
            pltpu.make_async_copy(q.at[0], q.at[0], qs_send.at[step]).wait()

        @pl.when(me < seq_n - 1)
        def _():
            pltpu.make_async_copy(vt.at[0], vt.at[0], ps_send.at[step]).wait()
            pltpu.make_async_copy(stat_out.at[0], stat_out.at[0], ss_send.at[step]).wait()

        piece = tok.at[0 : groups - 1, 0]
        pltpu.make_async_copy(piece, piece, o_send.at[step]).wait()
    piece = tbuf.at[pl.ds(0, rows_x - 1)]
    pltpu.make_async_copy(piece, piece, t_send).wait()
    for level in range(1, FAR_LEVELS):
        if level == 1:

            @pl.when(bit_of(level) == 0)
            def _():
                pltpu.make_async_copy(chip, chip, c_send.at[level]).wait()

        elif level <= low_levels:
            for own_bit in range(2):

                @pl.when(bit_of(level) == own_bit)
                def _():
                    piece = gat.at[pl.ds(0, rows_y // 2 - own_bit)]
                    pltpu.make_async_copy(piece, piece, c_send.at[level]).wait()

        else:

            @pl.when(bit_of(level) == 1)
            def _():
                piece = gat.at[pl.ds(0, rows_y - 1)]
                pltpu.make_async_copy(piece, piece, c_send.at[level]).wait()

        @pl.when(bit_of(level) == 1)
        def _():
            piece = bk.at[level, my_half, :]
            pltpu.make_async_copy(piece, piece, h_send.at[level]).wait()


def local(rows_x, rows_y, queries, key_vectors, values, level_weights, gate_branch, norm_gain):
    toks, width = queries.shape
    heads = width // HEAD_DIM
    groups = lax.axis_size("heads")
    out_rows, model = gate_branch.shape
    row_n = rows_y * 2
    part = heads * HEAD_DIM // row_n
    arrays = [queries, key_vectors, values, level_weights, gate_branch, norm_gain.reshape(1, -1)]
    dma = pltpu.SemaphoreType.DMA
    hbm = pl.BlockSpec(memory_space=pl.ANY)
    vmem = pl.BlockSpec(memory_space=pltpu.VMEM)
    head_shape = (heads, toks, HEAD_DIM)
    turned_shape = (heads, HEAD_DIM, toks)
    return pl.pallas_call(
        functools.partial(kernel, rows_x, rows_y, groups),
        out_shape=jax.ShapeDtypeStruct((out_rows, model), BF16),
        in_specs=[hbm] * 6,
        out_specs=vmem,
        scratch_shapes=[
            pltpu.VMEM(head_shape, BF16),
            pltpu.VMEM(head_shape, BF16),
            pltpu.VMEM(head_shape, BF16),
            pltpu.VMEM(turned_shape, BF16),
            pltpu.VMEM(head_shape, BF16),
            pltpu.VMEM(turned_shape, BF16),
            pltpu.VMEM(turned_shape, BF16),
            pltpu.VMEM((heads, 2, toks), F32),
            pltpu.VMEM((heads, 2, toks), F32),
            pltpu.VMEM(turned_shape, F32),
            pltpu.VMEM((heads, 2, toks), F32),
            pltpu.VMEM((heads, level_weights.shape[0], 1, toks), F32),
            pltpu.VMEM(gate_branch.shape, BF16),
            pltpu.VMEM(gate_branch.shape, F32),
            pltpu.VMEM(turned_shape, F32),
            pltpu.VMEM(head_shape, BF16),
            pltpu.VMEM((groups, heads, out_rows, HEAD_DIM), BF16),
            pltpu.VMEM((heads * HEAD_DIM, HEAD_DIM), BF16),
            pltpu.VMEM((heads * HEAD_DIM // 2, HEAD_DIM), BF16),
            pltpu.VMEM((heads * HEAD_DIM // 2, HEAD_DIM), BF16),
            pltpu.VMEM((rows_y, part, HEAD_DIM), BF16),
            pltpu.VMEM((rows_y // 2 - 1, part, HEAD_DIM), BF16),
            pltpu.VMEM((part, HEAD_DIM), F32),
            pltpu.VMEM((rows_x, part, HEAD_DIM), F32),
            pltpu.VMEM((2, part, HEAD_DIM), BF16),
            pltpu.VMEM((FAR_LEVELS, heads * HEAD_DIM, HEAD_DIM), BF16),
            pltpu.VMEM((1, model), F32),
            dma((heads,)),
            dma((heads,)),
            dma((heads,)),
            dma((heads,)),
            dma,
            dma,
            dma,
            dma,
            dma,
            dma,
            dma,
            dma,
            dma((heads,)),
            dma((heads,)),
            dma((heads,)),
            dma((heads,)),
            dma((heads,)),
            dma((heads,)),
            dma,
            dma,
            dma((FAR_LEVELS,)),
            dma((FAR_LEVELS,)),
            dma((FAR_LEVELS,)),
            dma((FAR_LEVELS,)),
            dma((heads,)),
            dma((heads,)),
            pltpu.SemaphoreType.REGULAR,
        ],
        compiler_params=pltpu.CompilerParams(
            collective_id=0, has_side_effects=True, vmem_limit_bytes=24 << 20
        ),
        name="layer",
    )(*[pltpu.with_memory_space_constraint(array, pltpu.HBM) for array in arrays])


def solution(mesh):
    rows_x, rows_y = 4, 8
    return jax.shard_map(
        functools.partial(local, rows_x, rows_y),
        mesh=mesh,
        in_specs=(
            P("seq", "heads"),
            P("seq", "heads"),
            P("seq", "heads"),
            P(None, "heads", "seq"),
            P(("seq", "heads"), None),
            P(),
        ),
        out_specs=P(("seq", "heads"), None),
        check_vma=False,
    )
```

```python
import functools
import math

import jax
import jax.numpy as jnp
from jax import lax
from jax.experimental import pallas as pl
from jax.experimental.pallas import tpu as pltpu
from jax.sharding import PartitionSpec as P

HEAD_DIM = 128
EPSILON = 1e-06
NEAR_LEVELS = 10
FAR_LEVELS = 6
TILE = 128
MESH = pl.DeviceIdType.MESH
F32 = jnp.float32
BF16 = jnp.bfloat16
SCALE = HEAD_DIM**-0.5
NEG = -1e30


def level_scale(level):
    return 2.0 ** (-0.5 * max(level - 1, 0))


def dot_nt(a, b):
    return lax.dot_general(a, b, (((1,), (1,)), ((), ())), preferred_element_type=F32)


def dot_nn(a, b):
    return jnp.dot(a, b, preferred_element_type=F32)


def kernel(
    rows_x,
    rows_y,
    groups,
    q_hbm,
    k_hbm,
    v_hbm,
    lw_hbm,
    gate_hbm,
    gain_hbm,
    out_ref,
    q,
    k,
    v,
    vt,
    qn,
    past_out,
    past_in,
    stat_out,
    stat_in,
    own_acc,
    own_stat,
    lw,
    gate,
    silu,
    acc,
    mix,
    tok,
    st,
    sib,
    chip,
    gat,
    bsrc,
    tsrc,
    tbuf,
    xsrc,
    bk,
    gain_ref,
    q_sem,
    k_sem,
    v_sem,
    lw_sem,
    gate_sem,
    gain_sem,
    s_send,
    s_recv,
    a_send,
    a_recv,
    z_send,
    z_recv,
    qs_send,
    qs_recv,
    ps_send,
    ps_recv,
    ss_send,
    ss_recv,
    t_send,
    t_recv,
    c_send,
    c_recv,
    h_send,
    h_recv,
    o_send,
    o_recv,
    here_sem,
):
    heads = k.shape[0]
    toks = k.shape[1]
    tiles = toks // TILE
    row_n = rows_y * 2
    seq_n = rows_x * row_n
    half = heads * HEAD_DIM // 2
    part = half // rows_y
    out_rows = toks // groups
    me = lax.axis_index("seq")
    zed = lax.axis_index("heads")
    x = me // row_n
    r = lax.rem(me, row_n)
    y = r // 2
    c = lax.rem(r, 2)

    def head_at(core, step):
        return lax.rem(core * (heads // 2) + step, heads)

    def bit_of(level):
        return lax.rem(me // (1 << level), 2)

    def row_id(place):
        return x * row_n + place

    barrier = pltpu.get_barrier_semaphore()
    greeted = (me > 0).astype(jnp.int32) + (me < seq_n - 1).astype(jnp.int32)
    for apart in (-1, 1):

        @pl.when((me + apart >= 0) & (me + apart < seq_n))
        def _():
            pl.semaphore_signal(
                barrier, inc=1, device_id={"seq": me + apart}, device_id_type=MESH
            )

    for step in (4, 3, 5, 2, 6, 1, 7):
        pl.semaphore_signal(
            barrier,
            inc=1,
            device_id={"seq": row_id(lax.rem(y + step, rows_y) * 2 + c)},
            device_id_type=MESH,
        )
        greeted += 1
    for step in range(1, rows_x):
        pl.semaphore_signal(
            barrier,
            inc=1,
            device_id={"seq": lax.rem(x + step, rows_x) * row_n + r},
            device_id_type=MESH,
        )
        greeted += 1
    for step in range(1, groups):

        @pl.when(zed + step < groups)
        def _():
            pl.semaphore_signal(
                barrier, inc=1, device_id={"heads": zed + step}, device_id_type=MESH
            )


    for h in range(heads):
        cols = pl.ds(h * HEAD_DIM, HEAD_DIM)
        pltpu.make_async_copy(v_hbm.at[:, cols], v.at[h], v_sem.at[h]).start()
        pltpu.make_async_copy(k_hbm.at[:, cols], k.at[h], k_sem.at[h]).start()
    for h in range(heads):
        cols = pl.ds(h * HEAD_DIM, HEAD_DIM)
        pltpu.make_async_copy(q_hbm.at[:, cols], q.at[h], q_sem.at[h]).start()
    lw_copies = [
        pltpu.make_async_copy(lw_hbm.at[:, pl.ds(h, 1), :], lw.at[h], lw_sem.at[h])
        for h in range(heads)
    ]
    for copy in lw_copies:
        copy.start()
    gate_copy = pltpu.make_async_copy(gate_hbm, gate, gate_sem)
    gate_copy.start()
    gain_copy = pltpu.make_async_copy(gain_hbm, gain_ref, gain_sem)
    gain_copy.start()

    for h in range(heads):
        pltpu.make_async_copy(k_hbm.at[:, pl.ds(0, HEAD_DIM)], k.at[h], k_sem.at[h]).wait()
        pltpu.make_async_copy(v_hbm.at[:, pl.ds(0, HEAD_DIM)], v.at[h], v_sem.at[h]).wait()
        st[pl.ds(h * HEAD_DIM, HEAD_DIM), :] = lax.dot_general(
            v[h], k[h], (((0,), (0,)), ((), ())), preferred_element_type=F32
        ).astype(BF16)

    pl.semaphore_wait(barrier, greeted + zed)
    for step in range(1, groups):

        @pl.when(zed >= step)
        def _():
            pl.semaphore_signal(
                here_sem, inc=1, device_id={"heads": zed - step}, device_id_type=MESH
            )


    sibling = me + 1 - 2 * c
    mine = pl.multiple_of(c * half + y * part, part)
    my_half = pl.ds(pl.multiple_of(c * half, half), half)
    other_half = pl.ds(pl.multiple_of((1 - c) * half, half), half)
    pltpu.make_async_remote_copy(
        st.at[other_half, :], sib, s_send, s_recv, device_id={"seq": sibling}, device_id_type=MESH
    ).start()

    def send_queries(step):
        h = head_at(c, step)

        @pl.when(me > 0)
        def _():
            pltpu.make_async_remote_copy(
                q.at[h],
                qn.at[h],
                qs_send.at[step],
                qs_recv.at[step],
                device_id={"seq": me - 1},
                device_id_type=MESH,
            ).start()

    for h in range(heads):
        pltpu.make_async_copy(q_hbm.at[:, pl.ds(0, HEAD_DIM)], q.at[h], q_sem.at[h]).wait()
    send_queries(0)

    @pl.when(c == 0)
    def _():
        pltpu.make_async_remote_copy(
            st, bk.at[0], z_send, z_recv, device_id={"seq": sibling}, device_id_type=MESH
        ).start()

    @pl.when(me == 0)
    def _():
        past_in[...] = jnp.zeros(past_in.shape, BF16)
        stat_in[...] = jnp.full(stat_in.shape, NEG, F32)

    @pl.when(c == 0)
    def _():
        bk[0] = jnp.zeros(bk.shape[1:], BF16)

    for level in range(1, FAR_LEVELS):

        @pl.when(bit_of(level) == 0)
        def _():
            bk[level] = jnp.zeros(bk.shape[1:], BF16)

    gate_copy.wait()
    gain_copy.wait()
    wide = gate[...].astype(F32)
    silu[...] = wide * jax.nn.sigmoid(wide)

    pltpu.make_async_copy(sib, sib, s_recv).wait()
    chip[...] = (st[my_half, :].astype(F32) + sib[...].astype(F32)).astype(BF16)
    for step in (4, 3, 5, 2, 6, 1, 7):
        place = lax.rem(y + step, rows_y)
        pltpu.make_async_remote_copy(
            chip.at[pl.ds(pl.multiple_of(place * part, part), part), :],
            gat.at[y],
            a_send,
            a_recv,
            device_id={"seq": row_id(place * 2 + c)},
            device_id_type=MESH,
        ).start()

    @pl.when(bit_of(1) == 0)
    def _():
        pltpu.make_async_remote_copy(
            chip,
            bk.at[1, my_half, :],
            c_send.at[1],
            c_recv.at[1],
            device_id={"seq": me + 2},
            device_id_type=MESH,
        ).start()

    gat[y] = chip[pl.ds(pl.multiple_of(y * part, part), part), :]
    send_queries(1)

    for copy in lw_copies:
        copy.wait()
    key_at = lax.broadcasted_iota(jnp.int32, (TILE, TILE), 0)
    query_at = lax.broadcasted_iota(jnp.int32, (TILE, TILE), 1)
    gain_exp = SCALE * math.log2(math.e)

    def within(step, carry):
        h = head_at(c, step)
        vt[h] = v[h].T
        causal = key_at <= query_at
        apart = key_at ^ query_at
        for i in range(tiles):
            cols = pl.ds(i * TILE, TILE)
            scores = dot_nt(k[h, pl.ds(0, (i + 1) * TILE), :], q[h, cols, :])
            parts = [scores[j * TILE : (j + 1) * TILE] for j in range(i + 1)]
            seen = parts[:-1] + [jnp.where(causal, parts[-1], NEG)]
            top = functools.reduce(jnp.maximum, seen)
            top = jnp.max(top, axis=0, keepdims=True) * gain_exp
            powers = [jnp.exp2(tile * gain_exp - top) for tile in seen]
            mass = jnp.sum(functools.reduce(jnp.add, powers), axis=0, keepdims=True)
            rows = [
                lw[h, level, :, cols] * (level_scale(level) * SCALE) for level in range(NEAR_LEVELS)
            ]
            near = [
                parts[j] * rows[TILE.bit_length() - 1 + (i ^ j).bit_length()] for j in range(i)
            ]
            mixed = jnp.broadcast_to(rows[0], (TILE, TILE))
            for level in range(1, TILE.bit_length()):
                mixed = jnp.where(apart >= 1 << (level - 1), rows[level], mixed)
            near.append(jnp.where(causal, parts[i] * mixed, 0.0))
            both = jnp.concatenate(
                [
                    jnp.concatenate([tile.astype(BF16) for tile in powers], axis=0),
                    jnp.concatenate([tile.astype(BF16) for tile in near], axis=0),
                ],
                axis=1,
            )
            found = dot_nn(vt[h, :, pl.ds(0, (i + 1) * TILE)], both)
            own_acc[h, :, cols] = found[:, :TILE]
            acc[h, :, cols] = found[:, TILE:]
            own_stat[h, 0:1, cols] = top
            own_stat[h, 1:2, cols] = mass
        return carry

    lax.fori_loop(0, heads, within, 0)

    def onward(step, carry):
        h = head_at(1 - c, step)
        pltpu.make_async_copy(q.at[h], qn.at[h], qs_recv.at[step]).wait()
        later = key_at > query_at
        for i in range(tiles):
            cols = pl.ds(i * TILE, TILE)
            count = tiles - i
            scores = dot_nt(k[h, pl.ds(i * TILE, count * TILE), :], qn[h, cols, :])
            parts = [scores[j * TILE : (j + 1) * TILE] for j in range(count)]
            seen = [jnp.where(later, parts[0], NEG)] + parts[1:]
            top = functools.reduce(jnp.maximum, seen)
            top = jnp.max(top, axis=0, keepdims=True) * gain_exp
            powers = [jnp.exp2(tile * gain_exp - top) for tile in seen]
            powers[0] = jnp.where(later, powers[0], 0.0)
            mass = jnp.sum(functools.reduce(jnp.add, powers), axis=0, keepdims=True)
            both = jnp.concatenate([tile.astype(BF16) for tile in powers], axis=0)
            found = dot_nn(vt[h, :, pl.ds(i * TILE, count * TILE)], both)
            past_out[h, :, cols] = found.astype(BF16)
            stat_out[h, 0:1, cols] = top
            stat_out[h, 1:2, cols] = mass
        for src, dst, send, recv in (
            (past_out, past_in, ps_send, ps_recv),
            (stat_out, stat_in, ss_send, ss_recv),
        ):
            pltpu.make_async_remote_copy(
                src.at[h],
                dst.at[h],
                send.at[step],
                recv.at[step],
                device_id={"seq": me + 1},
                device_id_type=MESH,
            ).start()
        return carry

    @pl.when(me < seq_n - 1)
    def _():
        onward(0, 0)

    pltpu.make_async_copy(
        gat.at[pl.ds(0, rows_y - 1)], gat.at[pl.ds(0, rows_y - 1)], a_recv
    ).wait()
    sums = [gat[i].astype(F32) for i in range(rows_y)]
    level_sums = []
    while len(sums) > 1:
        sums = [sums[2 * i] + sums[2 * i + 1] for i in range(len(sums) // 2)]
        level_sums.append(sums)
    low_levels = len(level_sums)
    firsts = {}
    count = 0
    for level, level_list in enumerate(level_sums[:-1], 2):
        firsts[level] = count
        for i in range(0, len(level_list), 2):
            bsrc[count] = level_list[i].astype(BF16)
            count += 1
    total = level_sums[-1][0]
    tsrc[...] = total
    tbuf[x] = total
    for step in range(1, rows_x):
        pltpu.make_async_remote_copy(
            tsrc,
            tbuf.at[x],
            t_send,
            t_recv,
            device_id={"seq": lax.rem(x + step, rows_x) * row_n + r},
            device_id_type=MESH,
        ).start()
    for level in range(low_levels, 1, -1):
        for step in (4, 3, 5, 2, 6, 1, 7, 0):
            place = lax.rem(y + step, rows_y)
            src = bsrc.at[firsts[level] + place // (1 << level)]
            dst = bk.at[level, pl.ds(mine, part), :]

            @pl.when(lax.rem(place // (1 << (level - 1)), 2) == 1)
            def _():
                if step == 0:
                    pltpu.make_async_copy(src, dst, c_recv.at[level]).start()
                else:
                    pltpu.make_async_remote_copy(
                        src,
                        dst,
                        c_send.at[level],
                        c_recv.at[level],
                        device_id={"seq": row_id(place * 2 + c)},
                        device_id_type=MESH,
                    ).start()

    send_queries(2)

    pltpu.make_async_copy(
        tbuf.at[pl.ds(0, rows_x - 1)], tbuf.at[pl.ds(0, rows_x - 1)], t_recv
    ).wait()
    xsrc[0] = tbuf[lax.max(x - 1, 0)].astype(BF16)
    xsrc[1] = (tbuf[0] + tbuf[1]).astype(BF16)
    for up in range(FAR_LEVELS - 1 - low_levels):
        level = low_levels + 1 + up

        @pl.when(bit_of(level) == 1)
        def _():
            for step in (4, 3, 5, 2, 6, 1, 7, 0):
                place = lax.rem(y + step, rows_y)
                src = xsrc.at[up]
                dst = bk.at[level, pl.ds(mine, part), :]
                if step == 0:
                    pltpu.make_async_copy(src, dst, c_recv.at[level]).start()
                else:
                    pltpu.make_async_remote_copy(
                        src,
                        dst,
                        c_send.at[level],
                        c_recv.at[level],
                        device_id={"seq": row_id(place * 2 + c)},
                        device_id_type=MESH,
                    ).start()

    send_queries(3)

    @pl.when(me < seq_n - 1)
    def _():
        lax.fori_loop(1, heads - 1, onward, 0)

    def take(level):
        @pl.when(bit_of(level) == 1)
        def _():
            piece = bk.at[level, my_half, :]
            pltpu.make_async_copy(piece, piece, c_recv.at[level]).wait()
            pltpu.make_async_remote_copy(
                piece,
                piece,
                h_send.at[level],
                h_recv.at[level],
                device_id={"seq": sibling},
                device_id_type=MESH,
            ).start()

    def take_other(level):
        @pl.when(bit_of(level) == 1)
        def _():
            piece = bk.at[level, other_half, :]
            pltpu.make_async_copy(piece, piece, h_recv.at[level]).wait()

    wide_cols = min(2 * TILE, toks)

    def far(h, cols, levels, found):
        rows = pl.ds(pl.multiple_of(h * HEAD_DIM, HEAD_DIM), HEAD_DIM)
        query = q[h, cols, :]
        for level in levels:
            weight = lw[h, NEAR_LEVELS + level, :, cols]
            weight = weight * (level_scale(NEAR_LEVELS + level) * SCALE)
            found += dot_nt(bk[level, rows, :], query) * weight
        return found

    def finish(step, carry):
        h = head_at(c, step)

        @pl.when(me > 0)
        def _():
            pltpu.make_async_copy(vt.at[h], past_in.at[h], ps_recv.at[step]).wait()
            pltpu.make_async_copy(stat_out.at[h], stat_in.at[h], ss_recv.at[step]).wait()

        for start in range(0, toks, wide_cols):
            cols = pl.ds(start, wide_cols)
            own_top = own_stat[h, 0:1, cols]
            past_top = stat_in[h, 0:1, cols]
            top = jnp.maximum(own_top, past_top)
            own_part = jnp.exp2(own_top - top)
            past_part = jnp.exp2(past_top - top)
            share = 1.0 / (own_part * own_stat[h, 1:2, cols] + past_part * stat_in[h, 1:2, cols])
            found = acc[h, :, cols] + own_acc[h, :, cols] * (own_part * share)
            found += past_in[h, :, cols].astype(F32) * (past_part * share)
            found = far(h, cols, range(FAR_LEVELS), found)
            mix[h, cols, :] = found.T.astype(BF16)
            for there in range(start // out_rows, (start + wide_cols) // out_rows):

                @pl.when(zed != there)
                def _():
                    pltpu.make_async_remote_copy(
                        mix.at[h, pl.ds(there * out_rows, out_rows), :],
                        tok.at[zed, h],
                        o_send.at[step],
                        o_recv.at[step],
                        device_id={"heads": there},
                        device_id_type=MESH,
                    ).start()

        tok[zed, h] = mix[h, pl.ds(pl.multiple_of(zed * out_rows, out_rows), out_rows), :]
        return carry

    for level in range(1, FAR_LEVELS):
        take(level)

    @pl.when(c == 1)
    def _():
        pltpu.make_async_copy(st, bk.at[0], z_recv).wait()

    @pl.when(zed < groups - 1)
    def _():
        pl.semaphore_wait(here_sem, groups - 1 - zed)

    lax.fori_loop(0, heads // 2, finish, 0)

    @pl.when(me < seq_n - 1)
    def _():
        onward(heads - 1, 0)

    for level in range(1, FAR_LEVELS):
        take_other(level)
    lax.fori_loop(heads // 2, heads, finish, 0)

    lanes = jnp.zeros((out_rows, HEAD_DIM), F32)
    for step in range(heads):
        piece = tok.at[0:groups - 1, 0]
        pltpu.make_async_copy(piece, piece, o_recv.at[step]).wait()
        h = head_at(c, step)
        for group in range(groups):
            cols = pl.ds(pl.multiple_of((group * heads + h) * HEAD_DIM, HEAD_DIM), HEAD_DIM)
            gated = tok[group, h].astype(F32) * silu[:, cols]
            silu[:, cols] = gated
            lanes += gated * gated
    square = jnp.sum(lanes, axis=1, keepdims=True) * (1.0 / (groups * heads * HEAD_DIM))
    inverse = lax.rsqrt(square + EPSILON)
    for index in range(groups * heads):
        cols = pl.ds(index * HEAD_DIM, HEAD_DIM)
        out_ref[:, cols] = (gain_ref[:, cols] * silu[:, cols] * inverse).astype(BF16)

    piece = gat.at[pl.ds(0, rows_y - 1)]
    pltpu.make_async_copy(piece, piece, a_send).wait()
    pltpu.make_async_copy(sib, sib, s_send).wait()

    @pl.when(c == 0)
    def _():
        pltpu.make_async_copy(st, st, z_send).wait()

    for step in range(heads):

        @pl.when(me > 0)
        def _():
            pltpu.make_async_copy(q.at[0], q.at[0], qs_send.at[step]).wait()

        @pl.when(me < seq_n - 1)
        def _():
            pltpu.make_async_copy(vt.at[0], vt.at[0], ps_send.at[step]).wait()
            pltpu.make_async_copy(stat_out.at[0], stat_out.at[0], ss_send.at[step]).wait()

        piece = tok.at[0 : groups - 1, 0]
        pltpu.make_async_copy(piece, piece, o_send.at[step]).wait()
    piece = tbuf.at[pl.ds(0, rows_x - 1)]
    pltpu.make_async_copy(piece, piece, t_send).wait()
    for level in range(1, FAR_LEVELS):
        if level == 1:

            @pl.when(bit_of(level) == 0)
            def _():
                pltpu.make_async_copy(chip, chip, c_send.at[level]).wait()

        elif level <= low_levels:
            for own_bit in range(2):

                @pl.when(bit_of(level) == own_bit)
                def _():
                    piece = gat.at[pl.ds(0, rows_y // 2 - own_bit)]
                    pltpu.make_async_copy(piece, piece, c_send.at[level]).wait()

        else:

            @pl.when(bit_of(level) == 1)
            def _():
                piece = gat.at[pl.ds(0, rows_y - 1)]
                pltpu.make_async_copy(piece, piece, c_send.at[level]).wait()

        @pl.when(bit_of(level) == 1)
        def _():
            piece = bk.at[level, my_half, :]
            pltpu.make_async_copy(piece, piece, h_send.at[level]).wait()


def local(rows_x, rows_y, queries, key_vectors, values, level_weights, gate_branch, norm_gain):
    toks, width = queries.shape
    heads = width // HEAD_DIM
    groups = lax.axis_size("heads")
    out_rows, model = gate_branch.shape
    row_n = rows_y * 2
    part = heads * HEAD_DIM // row_n
    arrays = [queries, key_vectors, values, level_weights, gate_branch, norm_gain.reshape(1, -1)]
    dma = pltpu.SemaphoreType.DMA
    hbm = pl.BlockSpec(memory_space=pl.ANY)
    vmem = pl.BlockSpec(memory_space=pltpu.VMEM)
    head_shape = (heads, toks, HEAD_DIM)
    turned_shape = (heads, HEAD_DIM, toks)
    return pl.pallas_call(
        functools.partial(kernel, rows_x, rows_y, groups),
        out_shape=jax.ShapeDtypeStruct((out_rows, model), BF16),
        in_specs=[hbm] * 6,
        out_specs=vmem,
        scratch_shapes=[
            pltpu.VMEM(head_shape, BF16),
            pltpu.VMEM(head_shape, BF16),
            pltpu.VMEM(head_shape, BF16),
            pltpu.VMEM(turned_shape, BF16),
            pltpu.VMEM(head_shape, BF16),
            pltpu.VMEM(turned_shape, BF16),
            pltpu.VMEM(turned_shape, BF16),
            pltpu.VMEM((heads, 2, toks), F32),
            pltpu.VMEM((heads, 2, toks), F32),
            pltpu.VMEM(turned_shape, F32),
            pltpu.VMEM((heads, 2, toks), F32),
            pltpu.VMEM((heads, level_weights.shape[0], 1, toks), F32),
            pltpu.VMEM(gate_branch.shape, BF16),
            pltpu.VMEM(gate_branch.shape, F32),
            pltpu.VMEM(turned_shape, F32),
            pltpu.VMEM(head_shape, BF16),
            pltpu.VMEM((groups, heads, out_rows, HEAD_DIM), BF16),
            pltpu.VMEM((heads * HEAD_DIM, HEAD_DIM), BF16),
            pltpu.VMEM((heads * HEAD_DIM // 2, HEAD_DIM), BF16),
            pltpu.VMEM((heads * HEAD_DIM // 2, HEAD_DIM), BF16),
            pltpu.VMEM((rows_y, part, HEAD_DIM), BF16),
            pltpu.VMEM((rows_y // 2 - 1, part, HEAD_DIM), BF16),
            pltpu.VMEM((part, HEAD_DIM), F32),
            pltpu.VMEM((rows_x, part, HEAD_DIM), F32),
            pltpu.VMEM((2, part, HEAD_DIM), BF16),
            pltpu.VMEM((FAR_LEVELS, heads * HEAD_DIM, HEAD_DIM), BF16),
            pltpu.VMEM((1, model), F32),
            dma((heads,)),
            dma((heads,)),
            dma((heads,)),
            dma((heads,)),
            dma,
            dma,
            dma,
            dma,
            dma,
            dma,
            dma,
            dma,
            dma((heads,)),
            dma((heads,)),
            dma((heads,)),
            dma((heads,)),
            dma((heads,)),
            dma((heads,)),
            dma,
            dma,
            dma((FAR_LEVELS,)),
            dma((FAR_LEVELS,)),
            dma((FAR_LEVELS,)),
            dma((FAR_LEVELS,)),
            dma((heads,)),
            dma((heads,)),
            pltpu.SemaphoreType.REGULAR,
        ],
        compiler_params=pltpu.CompilerParams(
            collective_id=0, has_side_effects=True, vmem_limit_bytes=24 << 20
        ),
        name="layer",
    )(*[pltpu.with_memory_space_constraint(array, pltpu.HBM) for array in arrays])


def solution(mesh):
    rows_x, rows_y = 4, 8
    return jax.shard_map(
        functools.partial(local, rows_x, rows_y),
        mesh=mesh,
        in_specs=(
            P("seq", "heads"),
            P("seq", "heads"),
            P("seq", "heads"),
            P(None, "heads", "seq"),
            P(("seq", "heads"), None),
            P(),
        ),
        out_specs=P(("seq", "heads"), None),
        check_vma=False,
    )
```

```python
import functools
import math

import jax
import jax.numpy as jnp
from jax import lax
from jax.experimental import pallas as pl
from jax.experimental.pallas import tpu as pltpu
from jax.sharding import PartitionSpec as P

HEAD_DIM = 128
EPSILON = 1e-06
NEAR_LEVELS = 10
FAR_LEVELS = 6
TILE = 128
MESH = pl.DeviceIdType.MESH
F32 = jnp.float32
BF16 = jnp.bfloat16
SCALE = HEAD_DIM**-0.5
NEG = -1e30


def level_scale(level):
    return 2.0 ** (-0.5 * max(level - 1, 0))


def dot_nt(a, b):
    return lax.dot_general(a, b, (((1,), (1,)), ((), ())), preferred_element_type=F32)


def dot_nn(a, b):
    return jnp.dot(a, b, preferred_element_type=F32)


def kernel(
    rows_x,
    rows_y,
    groups,
    q_hbm,
    k_hbm,
    v_hbm,
    lw_hbm,
    gate_hbm,
    gain_hbm,
    out_ref,
    q,
    k,
    v,
    vt,
    qn,
    past_out,
    past_in,
    stat_out,
    stat_in,
    own_acc,
    own_stat,
    lw,
    gate,
    silu,
    acc,
    mix,
    tok,
    st,
    sib,
    chip,
    gat,
    bsrc,
    tsrc,
    tbuf,
    xsrc,
    bk,
    gain_ref,
    q_sem,
    k_sem,
    v_sem,
    lw_sem,
    gate_sem,
    gain_sem,
    s_send,
    s_recv,
    a_send,
    a_recv,
    z_send,
    z_recv,
    qs_send,
    qs_recv,
    ps_send,
    ps_recv,
    ss_send,
    ss_recv,
    t_send,
    t_recv,
    c_send,
    c_recv,
    h_send,
    h_recv,
    o_send,
    o_recv,
    here_sem,
):
    heads = k.shape[0]
    toks = k.shape[1]
    tiles = toks // TILE
    row_n = rows_y * 2
    seq_n = rows_x * row_n
    half = heads * HEAD_DIM // 2
    part = half // rows_y
    out_rows = toks // groups
    me = lax.axis_index("seq")
    zed = lax.axis_index("heads")
    x = me // row_n
    r = lax.rem(me, row_n)
    y = r // 2
    c = lax.rem(r, 2)

    def head_at(core, step):
        return lax.rem(core * (heads // 2) + step, heads)

    def bit_of(level):
        return lax.rem(me // (1 << level), 2)

    def row_id(place):
        return x * row_n + place

    barrier = pltpu.get_barrier_semaphore()
    greeted = (me > 0).astype(jnp.int32) + (me < seq_n - 1).astype(jnp.int32)
    for apart in (-1, 1):

        @pl.when((me + apart >= 0) & (me + apart < seq_n))
        def _():
            pl.semaphore_signal(
                barrier, inc=1, device_id={"seq": me + apart}, device_id_type=MESH
            )

    for step in (4, 3, 5, 2, 6, 1, 7):
        pl.semaphore_signal(
            barrier,
            inc=1,
            device_id={"seq": row_id(lax.rem(y + step, rows_y) * 2 + c)},
            device_id_type=MESH,
        )
        greeted += 1
    for step in range(1, rows_x):
        pl.semaphore_signal(
            barrier,
            inc=1,
            device_id={"seq": lax.rem(x + step, rows_x) * row_n + r},
            device_id_type=MESH,
        )
        greeted += 1
    for step in range(1, groups):

        @pl.when(zed + step < groups)
        def _():
            pl.semaphore_signal(
                barrier, inc=1, device_id={"heads": zed + step}, device_id_type=MESH
            )


    for h in range(heads):
        cols = pl.ds(h * HEAD_DIM, HEAD_DIM)
        pltpu.make_async_copy(v_hbm.at[:, cols], v.at[h], v_sem.at[h]).start()
        pltpu.make_async_copy(k_hbm.at[:, cols], k.at[h], k_sem.at[h]).start()
    for h in range(heads):
        cols = pl.ds(h * HEAD_DIM, HEAD_DIM)
        pltpu.make_async_copy(q_hbm.at[:, cols], q.at[h], q_sem.at[h]).start()
    lw_copies = [
        pltpu.make_async_copy(lw_hbm.at[:, pl.ds(h, 1), :], lw.at[h], lw_sem.at[h])
        for h in range(heads)
    ]
    for copy in lw_copies:
        copy.start()
    gate_copy = pltpu.make_async_copy(gate_hbm, gate, gate_sem)
    gate_copy.start()
    gain_copy = pltpu.make_async_copy(gain_hbm, gain_ref, gain_sem)
    gain_copy.start()

    for h in range(heads):
        pltpu.make_async_copy(k_hbm.at[:, pl.ds(0, HEAD_DIM)], k.at[h], k_sem.at[h]).wait()
        pltpu.make_async_copy(v_hbm.at[:, pl.ds(0, HEAD_DIM)], v.at[h], v_sem.at[h]).wait()
        st[pl.ds(h * HEAD_DIM, HEAD_DIM), :] = lax.dot_general(
            v[h], k[h], (((0,), (0,)), ((), ())), preferred_element_type=F32
        ).astype(BF16)

    pl.semaphore_wait(barrier, greeted + zed)
    for step in range(1, groups):

        @pl.when(zed >= step)
        def _():
            pl.semaphore_signal(
                here_sem, inc=1, device_id={"heads": zed - step}, device_id_type=MESH
            )


    sibling = me + 1 - 2 * c
    mine = pl.multiple_of(c * half + y * part, part)
    my_half = pl.ds(pl.multiple_of(c * half, half), half)
    other_half = pl.ds(pl.multiple_of((1 - c) * half, half), half)
    pltpu.make_async_remote_copy(
        st.at[other_half, :], sib, s_send, s_recv, device_id={"seq": sibling}, device_id_type=MESH
    ).start()

    def send_queries(step):
        h = head_at(c, step)

        @pl.when(me > 0)
        def _():
            pltpu.make_async_remote_copy(
                q.at[h],
                qn.at[h],
                qs_send.at[step],
                qs_recv.at[step],
                device_id={"seq": me - 1},
                device_id_type=MESH,
            ).start()

    for h in range(heads):
        pltpu.make_async_copy(q_hbm.at[:, pl.ds(0, HEAD_DIM)], q.at[h], q_sem.at[h]).wait()
    send_queries(0)

    @pl.when(c == 0)
    def _():
        pltpu.make_async_remote_copy(
            st, bk.at[0], z_send, z_recv, device_id={"seq": sibling}, device_id_type=MESH
        ).start()

    @pl.when(me == 0)
    def _():
        past_in[...] = jnp.zeros(past_in.shape, BF16)
        stat_in[...] = jnp.full(stat_in.shape, NEG, F32)

    @pl.when(c == 0)
    def _():
        bk[0] = jnp.zeros(bk.shape[1:], BF16)

    for level in range(1, FAR_LEVELS):

        @pl.when(bit_of(level) == 0)
        def _():
            bk[level] = jnp.zeros(bk.shape[1:], BF16)

    gate_copy.wait()
    gain_copy.wait()
    wide = gate[...].astype(F32)
    silu[...] = wide * jax.nn.sigmoid(wide)

    pltpu.make_async_copy(sib, sib, s_recv).wait()
    chip[...] = (st[my_half, :].astype(F32) + sib[...].astype(F32)).astype(BF16)
    for step in (4, 3, 5, 2, 6, 1, 7):
        place = lax.rem(y + step, rows_y)
        pltpu.make_async_remote_copy(
            chip.at[pl.ds(pl.multiple_of(place * part, part), part), :],
            gat.at[y],
            a_send,
            a_recv,
            device_id={"seq": row_id(place * 2 + c)},
            device_id_type=MESH,
        ).start()

    @pl.when(bit_of(1) == 0)
    def _():
        pltpu.make_async_remote_copy(
            chip,
            bk.at[1, my_half, :],
            c_send.at[1],
            c_recv.at[1],
            device_id={"seq": me + 2},
            device_id_type=MESH,
        ).start()

    gat[y] = chip[pl.ds(pl.multiple_of(y * part, part), part), :]
    send_queries(1)

    for copy in lw_copies:
        copy.wait()
    key_at = lax.broadcasted_iota(jnp.int32, (TILE, TILE), 0)
    query_at = lax.broadcasted_iota(jnp.int32, (TILE, TILE), 1)
    gain_exp = SCALE * math.log2(math.e)

    def within(step, carry):
        h = head_at(c, step)
        vt[h] = v[h].T
        causal = key_at <= query_at
        apart = key_at ^ query_at
        for i in range(tiles):
            cols = pl.ds(i * TILE, TILE)
            scores = dot_nt(k[h, pl.ds(0, (i + 1) * TILE), :], q[h, cols, :])
            parts = [scores[j * TILE : (j + 1) * TILE] for j in range(i + 1)]
            seen = parts[:-1] + [jnp.where(causal, parts[-1], NEG)]
            top = functools.reduce(jnp.maximum, seen)
            top = jnp.max(top, axis=0, keepdims=True) * gain_exp
            powers = [jnp.exp2(tile * gain_exp - top) for tile in seen]
            mass = jnp.sum(functools.reduce(jnp.add, powers), axis=0, keepdims=True)
            rows = [
                lw[h, level, :, cols] * (level_scale(level) * SCALE) for level in range(NEAR_LEVELS)
            ]
            near = [
                parts[j] * rows[TILE.bit_length() - 1 + (i ^ j).bit_length()] for j in range(i)
            ]
            mixed = jnp.broadcast_to(rows[0], (TILE, TILE))
            for level in range(1, TILE.bit_length()):
                mixed = jnp.where(apart >= 1 << (level - 1), rows[level], mixed)
            near.append(jnp.where(causal, parts[i] * mixed, 0.0))
            both = jnp.concatenate(
                [
                    jnp.concatenate([tile.astype(BF16) for tile in powers], axis=0),
                    jnp.concatenate([tile.astype(BF16) for tile in near], axis=0),
                ],
                axis=1,
            )
            found = dot_nn(vt[h, :, pl.ds(0, (i + 1) * TILE)], both)
            own_acc[h, :, cols] = found[:, :TILE]
            acc[h, :, cols] = found[:, TILE:]
            own_stat[h, 0:1, cols] = top
            own_stat[h, 1:2, cols] = mass
        return carry

    lax.fori_loop(0, heads, within, 0)

    def onward(step, carry):
        h = head_at(1 - c, step)
        pltpu.make_async_copy(q.at[h], qn.at[h], qs_recv.at[step]).wait()
        later = key_at > query_at
        for i in range(tiles):
            cols = pl.ds(i * TILE, TILE)
            count = tiles - i
            scores = dot_nt(k[h, pl.ds(i * TILE, count * TILE), :], qn[h, cols, :])
            parts = [scores[j * TILE : (j + 1) * TILE] for j in range(count)]
            seen = [jnp.where(later, parts[0], NEG)] + parts[1:]
            top = functools.reduce(jnp.maximum, seen)
            top = jnp.max(top, axis=0, keepdims=True) * gain_exp
            powers = [jnp.exp2(tile * gain_exp - top) for tile in seen]
            powers[0] = jnp.where(later, powers[0], 0.0)
            mass = jnp.sum(functools.reduce(jnp.add, powers), axis=0, keepdims=True)
            both = jnp.concatenate([tile.astype(BF16) for tile in powers], axis=0)
            found = dot_nn(vt[h, :, pl.ds(i * TILE, count * TILE)], both)
            past_out[h, :, cols] = found.astype(BF16)
            stat_out[h, 0:1, cols] = top
            stat_out[h, 1:2, cols] = mass
        for src, dst, send, recv in (
            (past_out, past_in, ps_send, ps_recv),
            (stat_out, stat_in, ss_send, ss_recv),
        ):
            pltpu.make_async_remote_copy(
                src.at[h],
                dst.at[h],
                send.at[step],
                recv.at[step],
                device_id={"seq": me + 1},
                device_id_type=MESH,
            ).start()
        return carry

    @pl.when(r < row_n - 1)
    def _():
        onward(0, 0)

    pltpu.make_async_copy(
        gat.at[pl.ds(0, rows_y - 1)], gat.at[pl.ds(0, rows_y - 1)], a_recv
    ).wait()
    sums = [gat[i].astype(F32) for i in range(rows_y)]
    level_sums = []
    while len(sums) > 1:
        sums = [sums[2 * i] + sums[2 * i + 1] for i in range(len(sums) // 2)]
        level_sums.append(sums)
    low_levels = len(level_sums)
    firsts = {}
    count = 0
    for level, level_list in enumerate(level_sums[:-1], 2):
        firsts[level] = count
        for i in range(0, len(level_list), 2):
            bsrc[count] = level_list[i].astype(BF16)
            count += 1
    total = level_sums[-1][0]
    tsrc[...] = total
    tbuf[x] = total
    for step in range(1, rows_x):
        pltpu.make_async_remote_copy(
            tsrc,
            tbuf.at[x],
            t_send,
            t_recv,
            device_id={"seq": lax.rem(x + step, rows_x) * row_n + r},
            device_id_type=MESH,
        ).start()
    for level in range(low_levels, 1, -1):
        for step in (4, 3, 5, 2, 6, 1, 7, 0):
            place = lax.rem(y + step, rows_y)
            src = bsrc.at[firsts[level] + place // (1 << level)]
            dst = bk.at[level, pl.ds(mine, part), :]

            @pl.when(lax.rem(place // (1 << (level - 1)), 2) == 1)
            def _():
                if step == 0:
                    pltpu.make_async_copy(src, dst, c_recv.at[level]).start()
                else:
                    pltpu.make_async_remote_copy(
                        src,
                        dst,
                        c_send.at[level],
                        c_recv.at[level],
                        device_id={"seq": row_id(place * 2 + c)},
                        device_id_type=MESH,
                    ).start()

    send_queries(2)

    @pl.when((r == row_n - 1) & (me < seq_n - 1))
    def _():
        onward(0, 0)

    pltpu.make_async_copy(
        tbuf.at[pl.ds(0, rows_x - 1)], tbuf.at[pl.ds(0, rows_x - 1)], t_recv
    ).wait()
    xsrc[0] = tbuf[lax.max(x - 1, 0)].astype(BF16)
    xsrc[1] = (tbuf[0] + tbuf[1]).astype(BF16)
    for up in range(FAR_LEVELS - 1 - low_levels):
        level = low_levels + 1 + up

        @pl.when(bit_of(level) == 1)
        def _():
            for step in (4, 3, 5, 2, 6, 1, 7, 0):
                place = lax.rem(y + step, rows_y)
                src = xsrc.at[up]
                dst = bk.at[level, pl.ds(mine, part), :]
                if step == 0:
                    pltpu.make_async_copy(src, dst, c_recv.at[level]).start()
                else:
                    pltpu.make_async_remote_copy(
                        src,
                        dst,
                        c_send.at[level],
                        c_recv.at[level],
                        device_id={"seq": row_id(place * 2 + c)},
                        device_id_type=MESH,
                    ).start()

    send_queries(3)

    @pl.when(me < seq_n - 1)
    def _():
        lax.fori_loop(1, heads - 1, onward, 0)

    def take(level):
        @pl.when(bit_of(level) == 1)
        def _():
            piece = bk.at[level, my_half, :]
            pltpu.make_async_copy(piece, piece, c_recv.at[level]).wait()
            pltpu.make_async_remote_copy(
                piece,
                piece,
                h_send.at[level],
                h_recv.at[level],
                device_id={"seq": sibling},
                device_id_type=MESH,
            ).start()

    def take_other(level):
        @pl.when(bit_of(level) == 1)
        def _():
            piece = bk.at[level, other_half, :]
            pltpu.make_async_copy(piece, piece, h_recv.at[level]).wait()

    wide_cols = min(2 * TILE, toks)

    def far(h, cols, levels, found):
        rows = pl.ds(pl.multiple_of(h * HEAD_DIM, HEAD_DIM), HEAD_DIM)
        query = q[h, cols, :]
        for level in levels:
            weight = lw[h, NEAR_LEVELS + level, :, cols]
            weight = weight * (level_scale(NEAR_LEVELS + level) * SCALE)
            found += dot_nt(bk[level, rows, :], query) * weight
        return found

    def gather(step):
        h = head_at(c, step)

        @pl.when(me > 0)
        def _():
            pltpu.make_async_copy(vt.at[h], past_in.at[h], ps_recv.at[step]).wait()
            pltpu.make_async_copy(stat_out.at[h], stat_in.at[h], ss_recv.at[step]).wait()

        for start in range(0, toks, wide_cols):
            cols = pl.ds(start, wide_cols)
            own_top = own_stat[h, 0:1, cols]
            past_top = stat_in[h, 0:1, cols]
            top = jnp.maximum(own_top, past_top)
            own_part = jnp.exp2(own_top - top)
            past_part = jnp.exp2(past_top - top)
            share = 1.0 / (own_part * own_stat[h, 1:2, cols] + past_part * stat_in[h, 1:2, cols])
            found = acc[h, :, cols] + own_acc[h, :, cols] * (own_part * share)
            found += past_in[h, :, cols].astype(F32) * (past_part * share)
            acc[h, :, cols] = far(h, cols, range(low_levels + 1), found)

    def finish(step):
        h = head_at(c, step)
        for start in range(0, toks, wide_cols):
            cols = pl.ds(start, wide_cols)
            found = far(h, cols, range(low_levels + 1, FAR_LEVELS), acc[h, :, cols])
            mix[h, cols, :] = found.T.astype(BF16)
            for there in range(start // out_rows, (start + wide_cols) // out_rows):

                @pl.when(zed != there)
                def _():
                    pltpu.make_async_remote_copy(
                        mix.at[h, pl.ds(there * out_rows, out_rows), :],
                        tok.at[zed, h],
                        o_send.at[step],
                        o_recv.at[step],
                        device_id={"heads": there},
                        device_id_type=MESH,
                    ).start()

        tok[zed, h] = mix[h, pl.ds(pl.multiple_of(zed * out_rows, out_rows), out_rows), :]

    def whole(step, carry):
        gather(step)
        finish(step)
        return carry

    @pl.when(zed < groups - 1)
    def _():
        pl.semaphore_wait(here_sem, groups - 1 - zed)

    for level in range(1, low_levels + 1):
        take(level)

    @pl.when(c == 1)
    def _():
        pltpu.make_async_copy(st, bk.at[0], z_recv).wait()

    gather(0)
    for level in range(low_levels + 1, FAR_LEVELS):
        take(level)
    finish(0)
    lax.fori_loop(1, heads // 2, whole, 0)

    @pl.when(me < seq_n - 1)
    def _():
        onward(heads - 1, 0)

    for level in range(1, FAR_LEVELS):
        take_other(level)
    lax.fori_loop(heads // 2, heads, whole, 0)

    lanes = jnp.zeros((out_rows, HEAD_DIM), F32)
    for step in range(heads):
        piece = tok.at[0:groups - 1, 0]
        pltpu.make_async_copy(piece, piece, o_recv.at[step]).wait()
        h = head_at(c, step)
        for group in range(groups):
            cols = pl.ds(pl.multiple_of((group * heads + h) * HEAD_DIM, HEAD_DIM), HEAD_DIM)
            gated = tok[group, h].astype(F32) * silu[:, cols]
            silu[:, cols] = gated
            lanes += gated * gated
    square = jnp.sum(lanes, axis=1, keepdims=True) * (1.0 / (groups * heads * HEAD_DIM))
    inverse = lax.rsqrt(square + EPSILON)
    for index in range(groups * heads):
        cols = pl.ds(index * HEAD_DIM, HEAD_DIM)
        out_ref[:, cols] = (gain_ref[:, cols] * silu[:, cols] * inverse).astype(BF16)

    piece = gat.at[pl.ds(0, rows_y - 1)]
    pltpu.make_async_copy(piece, piece, a_send).wait()
    pltpu.make_async_copy(sib, sib, s_send).wait()

    @pl.when(c == 0)
    def _():
        pltpu.make_async_copy(st, st, z_send).wait()

    for step in range(heads):

        @pl.when(me > 0)
        def _():
            pltpu.make_async_copy(q.at[0], q.at[0], qs_send.at[step]).wait()

        @pl.when(me < seq_n - 1)
        def _():
            pltpu.make_async_copy(vt.at[0], vt.at[0], ps_send.at[step]).wait()
            pltpu.make_async_copy(stat_out.at[0], stat_out.at[0], ss_send.at[step]).wait()

        piece = tok.at[0 : groups - 1, 0]
        pltpu.make_async_copy(piece, piece, o_send.at[step]).wait()
    piece = tbuf.at[pl.ds(0, rows_x - 1)]
    pltpu.make_async_copy(piece, piece, t_send).wait()
    for level in range(1, FAR_LEVELS):
        if level == 1:

            @pl.when(bit_of(level) == 0)
            def _():
                pltpu.make_async_copy(chip, chip, c_send.at[level]).wait()

        elif level <= low_levels:
            for own_bit in range(2):

                @pl.when(bit_of(level) == own_bit)
                def _():
                    piece = gat.at[pl.ds(0, rows_y // 2 - own_bit)]
                    pltpu.make_async_copy(piece, piece, c_send.at[level]).wait()

        else:

            @pl.when(bit_of(level) == 1)
            def _():
                piece = gat.at[pl.ds(0, rows_y - 1)]
                pltpu.make_async_copy(piece, piece, c_send.at[level]).wait()

        @pl.when(bit_of(level) == 1)
        def _():
            piece = bk.at[level, my_half, :]
            pltpu.make_async_copy(piece, piece, h_send.at[level]).wait()


def local(rows_x, rows_y, queries, key_vectors, values, level_weights, gate_branch, norm_gain):
    toks, width = queries.shape
    heads = width // HEAD_DIM
    groups = lax.axis_size("heads")
    out_rows, model = gate_branch.shape
    row_n = rows_y * 2
    part = heads * HEAD_DIM // row_n
    arrays = [queries, key_vectors, values, level_weights, gate_branch, norm_gain.reshape(1, -1)]
    dma = pltpu.SemaphoreType.DMA
    hbm = pl.BlockSpec(memory_space=pl.ANY)
    vmem = pl.BlockSpec(memory_space=pltpu.VMEM)
    head_shape = (heads, toks, HEAD_DIM)
    turned_shape = (heads, HEAD_DIM, toks)
    return pl.pallas_call(
        functools.partial(kernel, rows_x, rows_y, groups),
        out_shape=jax.ShapeDtypeStruct((out_rows, model), BF16),
        in_specs=[hbm] * 6,
        out_specs=vmem,
        scratch_shapes=[
            pltpu.VMEM(head_shape, BF16),
            pltpu.VMEM(head_shape, BF16),
            pltpu.VMEM(head_shape, BF16),
            pltpu.VMEM(turned_shape, BF16),
            pltpu.VMEM(head_shape, BF16),
            pltpu.VMEM(turned_shape, BF16),
            pltpu.VMEM(turned_shape, BF16),
            pltpu.VMEM((heads, 2, toks), F32),
            pltpu.VMEM((heads, 2, toks), F32),
            pltpu.VMEM(turned_shape, F32),
            pltpu.VMEM((heads, 2, toks), F32),
            pltpu.VMEM((heads, level_weights.shape[0], 1, toks), F32),
            pltpu.VMEM(gate_branch.shape, BF16),
            pltpu.VMEM(gate_branch.shape, F32),
            pltpu.VMEM(turned_shape, F32),
            pltpu.VMEM(head_shape, BF16),
            pltpu.VMEM((groups, heads, out_rows, HEAD_DIM), BF16),
            pltpu.VMEM((heads * HEAD_DIM, HEAD_DIM), BF16),
            pltpu.VMEM((heads * HEAD_DIM // 2, HEAD_DIM), BF16),
            pltpu.VMEM((heads * HEAD_DIM // 2, HEAD_DIM), BF16),
            pltpu.VMEM((rows_y, part, HEAD_DIM), BF16),
            pltpu.VMEM((rows_y // 2 - 1, part, HEAD_DIM), BF16),
            pltpu.VMEM((part, HEAD_DIM), F32),
            pltpu.VMEM((rows_x, part, HEAD_DIM), F32),
            pltpu.VMEM((2, part, HEAD_DIM), BF16),
            pltpu.VMEM((FAR_LEVELS, heads * HEAD_DIM, HEAD_DIM), BF16),
            pltpu.VMEM((1, model), F32),
            dma((heads,)),
            dma((heads,)),
            dma((heads,)),
            dma((heads,)),
            dma,
            dma,
            dma,
            dma,
            dma,
            dma,
            dma,
            dma,
            dma((heads,)),
            dma((heads,)),
            dma((heads,)),
            dma((heads,)),
            dma((heads,)),
            dma((heads,)),
            dma,
            dma,
            dma((FAR_LEVELS,)),
            dma((FAR_LEVELS,)),
            dma((FAR_LEVELS,)),
            dma((FAR_LEVELS,)),
            dma((heads,)),
            dma((heads,)),
            pltpu.SemaphoreType.REGULAR,
        ],
        compiler_params=pltpu.CompilerParams(
            collective_id=0, has_side_effects=True, vmem_limit_bytes=24 << 20
        ),
        name="layer",
    )(*[pltpu.with_memory_space_constraint(array, pltpu.HBM) for array in arrays])


def solution(mesh):
    rows_x, rows_y = 4, 8
    return jax.shard_map(
        functools.partial(local, rows_x, rows_y),
        mesh=mesh,
        in_specs=(
            P("seq", "heads"),
            P("seq", "heads"),
            P("seq", "heads"),
            P(None, "heads", "seq"),
            P(("seq", "heads"), None),
            P(),
        ),
        out_specs=P(("seq", "heads"), None),
        check_vma=False,
    )
```
